32 devices in a mesh: probe: 16 (over z, x, core), depth: 2 (over y).
Axes of the slice: x: 2, y: 2, z: 4, core: 2. Of those that a mesh axis runs over, the one named last changes fastest.
Arguments:
- potential: float32 [4, 2048, 1024], P('depth', 'probe'), may hold values from -6 to 6
- probe: float32 [2, 256, 256], replicated, may hold values from -6 to 6
- positions: int32 [16, 2], P('probe'), may hold values from 0 to 2047, as said below
- intensity: float32 [16, 256, 256], P('probe'), may hold values from 0 to 4
Outputs:
- potential_grad: float32 [4, 2048, 1024], P('depth', 'probe')
The draws below stay inside these ranges and needn't reach their ends.
Inputs may be any that keep to these rules, and one draw needn't show every extreme that they name: `positions`: entry 0 of probe p is the top row of its window and entry 1 its left column, 0 to 768. The window's centre row, (entry 128) mod 2048, lies in rows g * 128 to g * 128 + 127, where g = p // 1 is the probe's group.
All inputs are finite; a program needn't handle non-finite values.
Results may differ from the reference program's by a relative error of at most 0.0003.
Values sent between devices are 32-bit elements; how exact they have to be, the bound alone decides.
No kernel may reach another device: no remote copies, remote signals or barrier semaphores. Data moves between devices by JAX's collectives and lax.ppermute only.
A program may use at most 64 MiB of HBM per device.

```python
import jax
import jax.numpy as jnp
from jax import lax

W = 256
PR_DEV = 1
NY = 1024
STRIP = 128
NX = 2048
SLICES = 4
PROBES = 16


def draw_positions(key, part):
    first_key = jax.random.fold_in(key, 11)
    second_key = jax.random.fold_in(key, 23)
    probe_ids = jnp.arange(PROBES, dtype=jnp.int32)
    group_ids = probe_ids // PR_DEV
    within = probe_ids % PR_DEV
    offsets = jax.random.randint(first_key, (PROBES,), 0, STRIP, dtype=jnp.int32)
    offsets = offsets.at[0].set(STRIP - 1).at[PR_DEV].set(0)
    row_tops = (group_ids * STRIP + offsets - STRIP) % NX
    spacing = max(PR_DEV - 1, 1)
    base = within * (NY - W) // spacing
    jitter = jax.random.randint(second_key, (PROBES,), -(W // 8), W // 8 + 1, dtype=jnp.int32)
    column_lefts = jnp.clip(base + jitter, 0, NY - W)
    column_lefts = column_lefts.at[1].set(0).at[PROBES - 1].set(NY - W)
    return jnp.stack([row_tops, column_lefts], axis=1).astype(jnp.int32)


def block_scale(own_key, shape, split, least, high):
    gain, own = 1.0, jax.random.fold_in(own_key, 6)
    for dim, shards_of in split:
        heights = jnp.exp(jax.random.uniform(jax.random.fold_in(own, dim), (shards_of,), jnp.float32, least / len(split), high / len(split)))
        gain = gain * jnp.repeat(heights, shape[dim] // shards_of).reshape([-1 if axis == dim else 1 for axis in range(len(shape))])
    return gain


def bell_draw(own_key, shape, spread, reach, pieces=(), kind=jnp.bfloat16):
    drawn = jax.random.normal(own_key, shape, jnp.float32) * spread
    if len(pieces) > 0:
        drawn = block_scale(own_key, shape, pieces, -0.22, 0.18) * drawn
    return jnp.clip(drawn, min=-reach, max=reach).astype(kind)


def setup_inputs(seed: int = 0) -> dict:
    streams_of = jax.random.split(jax.random.key(seed), 5)
    return {
        "potential": bell_draw(streams_of[0], (SLICES, NX, NY), 1.0, 6.0, ((0, 2), (1, 16)), jnp.float32),
        "probe": bell_draw(streams_of[1], (2, W, W), 1.0, 6.0, (), jnp.float32),
        "positions": draw_positions(jax.random.fold_in(streams_of[4], 71), 0),
        "intensity": jnp.clip(4.0 * jax.random.uniform(streams_of[3], (PROBES, W, W), jnp.float32) ** block_scale(streams_of[3], (PROBES, W, W), ((0, 16),), -0.2, 0.2), 0.0, 4.0),
    }


interaction = 0.5
fresnel_phase = 60.0
highest = lax.Precision.HIGHEST

def dft_tables(extent):
    counter = jnp.arange(extent, dtype=jnp.int32)
    product = counter[:, None] * counter[None, :] % extent
    angles = 2.0 * jnp.pi / extent * product.astype(jnp.float32)
    norm_scale = 1.0 / jnp.sqrt(jnp.float32(extent))
    return (jnp.cos(angles) * norm_scale, -jnp.sin(angles) * norm_scale)

def kernel_table(extent):
    counter = jnp.arange(extent, dtype=jnp.int32)
    frequency = ((counter + extent // 2) % extent - extent // 2).astype(jnp.float32) / extent
    phases = -fresnel_phase * (frequency[:, None] ** 2 + frequency[None, :] ** 2)
    return (jnp.cos(phases), jnp.sin(phases))

def left_product(matrix, field):
    return jnp.einsum('jk,...kl->...jl', matrix, field, precision=highest)

def right_product(field, matrix):
    return jnp.einsum('...jk,kl->...jl', field, matrix, precision=highest)

def complex_left(matrices, fields):
    return (left_product(matrices[0], fields[0]) - left_product(matrices[1], fields[1]), left_product(matrices[0], fields[1]) + left_product(matrices[1], fields[0]))

def complex_right(fields, matrices):
    return (right_product(fields[0], matrices[0]) - right_product(fields[1], matrices[1]), right_product(fields[0], matrices[1]) + right_product(fields[1], matrices[0]))

def forward_dft(fields, tables):
    return complex_right(complex_left(tables, fields), tables)

def inverse_dft(fields, tables):
    conjugate = (tables[0], -tables[1])
    return complex_right(complex_left(conjugate, fields), conjugate)

def propagate(fields, tables, kernel):
    spectrum = forward_dft(fields, tables)
    moved = (kernel[0] * spectrum[0] - kernel[1] * spectrum[1], kernel[0] * spectrum[1] + kernel[1] * spectrum[0])
    return inverse_dft(moved, tables)

def transmit(fields, window):
    cosine = jnp.cos(interaction * window)
    sine_part = jnp.sin(interaction * window)
    return (cosine * fields[0] - sine_part * fields[1], cosine * fields[1] + sine_part * fields[0])

def probe_loss(windows, probe, measured, tables, kernel):
    fields = (probe[0], probe[1])
    for layer_id in range(windows.shape[0]):
        fields = propagate(transmit(fields, windows[layer_id]), tables, kernel)
    far_field = forward_dft(fields, tables)
    misfit = far_field[0] * far_field[0] + far_field[1] * far_field[1] - measured
    return 0.25 * jnp.sum(misfit * misfit)

def reference(potential, probe, positions, intensity):
    tables = dft_tables(W)
    kernel = kernel_table(W)
    offsets = jnp.arange(W, dtype=jnp.int32)
    grad_window = jax.grad(probe_loss)

    def one_probe(entry_pair):
        location, measured = entry_pair
        row_ids = ((location[0] + offsets) % NX).astype(jnp.int32)
        row_band = jnp.take(potential, row_ids, axis=1)
        windows = lax.dynamic_slice_in_dim(row_band, location[1].astype(jnp.int32), W, 2)
        return grad_window(windows, probe, measured, tables, kernel)
    window_grads = lax.map(one_probe, (positions, intensity))

    def accumulate(running, entry_pair):
        location, window_grad = entry_pair
        row_ids = ((location[0] + offsets) % NX).astype(jnp.int32)
        column_ids = (location[1] + offsets).astype(jnp.int32)
        return (running.at[:, row_ids[:, None], column_ids[None, :]].add(window_grad), None)
    running, unused = lax.scan(accumulate, jnp.zeros_like(potential), (positions, window_grads))
    return running
```

```python
import functools

import jax
import jax.numpy as jnp
import numpy as np
from jax import lax
from jax.experimental import pallas as pl
from jax.experimental.pallas import tpu as pltpu
from jax.sharding import PartitionSpec as P

interaction = 0.5
fresnel_phase = 60.0
f32 = jnp.float32
bf16 = jnp.bfloat16

VMEM = pl.BlockSpec(memory_space=pltpu.VMEM)
SMEM = pl.BlockSpec(memory_space=pltpu.SMEM)


def poly_tables():
    x = np.cos(np.linspace(0.0, np.pi / 2, 4001)) * (np.pi / 2) * 1.0005
    z = x * x
    fit = np.polynomial.chebyshev.Chebyshev.fit
    kind = np.polynomial.Polynomial
    sine = fit(z, np.sinc(x / np.pi), 5).convert(kind=kind).coef
    cosine = fit(z, np.cos(x), 5).convert(kind=kind).coef
    return [float(v) for v in sine], [float(v) for v in cosine]


def split_table(matrix):
    parts = []
    for real in (matrix.real, matrix.imag, -matrix.imag):
        wide = real.astype(np.float32)
        high = wide.astype(bf16)
        parts.append(high)
        parts.append((real - high.astype(np.float64)).astype(np.float32).astype(bf16))
    return np.stack(parts)


def tables(extent):
    index = np.arange(extent)
    dft = np.exp(-2j * np.pi * ((index[:, None] * index[None, :]) % extent) / extent)
    dft = dft / np.sqrt(extent)
    frequency = ((index + extent // 2) % extent - extent // 2) / extent
    chirp = np.exp(-1j * fresnel_phase * frequency**2)
    propagator = np.conj(dft) @ (chirp[:, None] * dft)
    return split_table(propagator), split_table(dft)


def sin_cos(window):
    sine, cosine = poly_tables()
    half = window * (interaction / 2)
    turns = jnp.round(half * (1.0 / np.pi))
    pi_high = float(np.float32(3.140625))
    pi_low = float(np.pi - 3.140625)
    x = (half - turns * pi_high) - turns * pi_low
    z = x * x
    s = sine[5]
    c = cosine[5]
    for k in range(4, -1, -1):
        s = s * z + sine[k]
        c = c * z + cosine[k]
    s = s * x
    return 2.0 * s * c, 1.0 - 2.0 * (s * s)


def columns_of(ref, layer, column):
    extent = 2 * ref.shape[1]
    block = column // extent
    last = ref.shape[2] // extent - 1
    low = ref[layer, :, pl.ds(pl.multiple_of(block * extent, extent), extent)]
    after = jnp.minimum(block + 1, last)
    high = ref[layer, :, pl.ds(pl.multiple_of(after * extent, extent), extent)]
    lane = lax.broadcasted_iota(jnp.int32, low.shape, 1)
    return jnp.where(lane >= column % extent, low, high)


def cut_kernel(*refs):
    count = (len(refs) - 1) // 2
    potential = refs[count]
    for k in range(count):
        for layer in range(potential.shape[0]):
            refs[count + 1 + k][layer] = columns_of(potential, layer, refs[k][0, 1])


def cut(potential, *positions):
    layers, strip, _ = potential.shape
    shape = jax.ShapeDtypeStruct((layers, strip, 2 * strip), f32)
    return pl.pallas_call(
        cut_kernel,
        out_shape=[shape] * len(positions),
        in_specs=[SMEM] * len(positions) + [VMEM],
        out_specs=[VMEM] * len(positions),
        name="cut",
    )(*positions, potential)


def merge_kernel(position, own, above, below, out):
    layers, strip, _ = own.shape
    local_row = position[0, 0] % strip
    for layer in range(layers):
        out[layer, :strip] = own[layer]
        row = lax.broadcasted_iota(jnp.int32, own.shape[1:], 0)
        out[layer, strip:] = jnp.where(row >= local_row, above[layer], below[layer])


def merge(position, own, above, below):
    layers, strip, extent = own.shape
    return pl.pallas_call(
        merge_kernel,
        out_shape=jax.ShapeDtypeStruct((layers, extent, extent), f32),
        in_specs=[SMEM] + [VMEM] * 3,
        out_specs=VMEM,
        name="merge",
    )(position, own, above, below)


def parts_of(x):
    high = x.astype(bf16)
    return high, (x - high.astype(f32)).astype(bf16)


def dot(a, b):
    return jnp.dot(a, b, preferred_element_type=f32)


def sandwich(m, real, imag):
    m = [m[k] for k in range(6)]
    rows = jnp.concatenate
    rh, rl = parts_of(real)
    ih, il = parts_of(imag)
    left = rows([rh, rl, rh, ih, il, ih], axis=1)
    yr = dot(left, rows([m[0], m[0], m[1], m[4], m[4], m[5]], axis=0))
    yi = dot(left, rows([m[2], m[2], m[3], m[0], m[0], m[1]], axis=0))
    rh, rl = parts_of(yr)
    ih, il = parts_of(yi)
    right = rows([rh, rl, rh, ih, il, ih], axis=0)
    zr = dot(rows([m[0], m[0], m[1], m[4], m[4], m[5]], axis=1), right)
    zi = dot(rows([m[2], m[2], m[3], m[0], m[0], m[1]], axis=1), right)
    return zr, zi


def solve_kernel(depth_count, place, position, probe, intensity, prop, dft, *refs):
    blocks = refs[:depth_count]
    out, trans, saved = refs[depth_count:]
    layers, extent, _ = out.shape
    strip = extent // 2
    slices = layers * depth_count
    depth = place[0]
    for k in range(depth_count):
        owner = (depth - k + depth_count) % depth_count
        for layer in range(layers):
            s, c = sin_cos(blocks[k][layer])
            trans[owner * layers + layer, 0] = c
            trans[owner * layers + layer, 1] = s

    row_shift = position[0, 0] % strip + strip
    column_shift = position[0, 1] % extent

    def rolled(x):
        return pltpu.roll(pltpu.roll(x, row_shift, 0), column_shift, 1)

    def transmit(s, real, imag):
        c = trans[s, 0]
        t = trans[s, 1]
        return c * real - t * imag, c * imag + t * real

    def forward(s, wave):
        real, imag = transmit(s, *wave)
        saved[s, 0] = real
        saved[s, 1] = imag
        return sandwich(prop, real, imag)

    wave = (rolled(probe[0]), rolled(probe[1]))
    wave = lax.fori_loop(0, slices - 1, forward, wave)
    real, imag = transmit(slices - 1, *wave)
    saved[slices - 1, 0] = real
    saved[slices - 1, 1] = imag
    far_real, far_imag = sandwich(dft, real, imag)
    misfit = far_real * far_real + far_imag * far_imag - intensity[0]
    wave = sandwich(dft, misfit * far_real, -(misfit * far_imag))

    def term(s, wave):
        @pl.when(s < (depth + 1) * layers)
        def _():
            real = saved[s, 0]
            imag = saved[s, 1]
            out[s - depth * layers] = -interaction * (wave[1] * real + wave[0] * imag)

    term(slices - 1, wave)

    def backward(step, wave):
        s = slices - 1 - step
        real, imag = transmit(s, *wave)
        wave = sandwich(prop, real, imag)
        term(s - 1, wave)
        return wave

    lax.fori_loop(0, slices - 1 - depth * layers, backward, wave)


def solve(place, position, probe, intensity, blocks):
    layers, extent, _ = blocks[0].shape
    count = len(blocks)
    slices = layers * count
    prop, dft = tables(extent)
    return pl.pallas_call(
        functools.partial(solve_kernel, count),
        out_shape=jax.ShapeDtypeStruct((layers, extent, extent), f32),
        in_specs=[SMEM] * 2 + [VMEM] * (4 + count),
        out_specs=VMEM,
        scratch_shapes=[pltpu.VMEM((slices, 2, extent, extent), f32)] * 2,
        compiler_params=pltpu.CompilerParams(vmem_limit_bytes=56 * 2**20),
        name="solve",
    )(place, position, probe, intensity, jnp.asarray(prop), jnp.asarray(dft), *blocks)


def place_kernel(position, before, after, own, from_before, from_after, out):
    layers, strip, columns = out.shape
    extent = 2 * strip
    row = lax.broadcasted_iota(jnp.int32, (strip, extent), 0)
    lane = lax.broadcasted_iota(jnp.int32, (strip, extent), 1)

    def covered(column, block):
        global_column = lane + block * extent
        return (global_column >= column) & (global_column < column + extent)

    below = row < before[0, 0] % strip
    above = row >= after[0, 0] % strip
    for block in range(columns // extent):
        mine = covered(position[0, 1], block)
        low = covered(before[0, 1], block) & below
        high = covered(after[0, 1], block) & above
        for layer in range(layers):
            value = jnp.where(mine, own[layer, :strip], 0.0)
            value = value + jnp.where(low, from_before[layer], 0.0)
            value = value + jnp.where(high, from_after[layer], 0.0)
            out[layer, :, block * extent : (block + 1) * extent] = value


def local(potential, probe, positions, intensity):
    layers, strip, columns = potential.shape
    extent = probe.shape[1]
    assert positions.shape[0] == 1 and extent == 2 * strip and columns % extent == 0
    count = lax.axis_size("probe")
    depth_count = lax.axis_size("depth")
    forward = [(i, (i + 1) % count) for i in range(count)]
    backward = [(i, (i - 1) % count) for i in range(count)]
    before = lax.ppermute(positions, "probe", forward)
    after = lax.ppermute(positions, "probe", backward)
    (own,) = cut(potential, positions)
    for_after, for_before = cut(potential, after, before)
    above = lax.ppermute(for_after, "probe", forward)
    below = lax.ppermute(for_before, "probe", backward)
    window = merge(positions, own, above, below)
    blocks = [window]
    for k in range(1, depth_count):
        pairs = [(i, (i + k) % depth_count) for i in range(depth_count)]
        blocks.append(lax.ppermute(window, "depth", pairs))
    place = lax.axis_index("depth").astype(jnp.int32).reshape(1)
    terms = solve(place, positions, probe, intensity, blocks)
    other = terms[:, strip:]
    from_before = lax.ppermute(other, "probe", forward)
    from_after = lax.ppermute(other, "probe", backward)
    return pl.pallas_call(
        place_kernel,
        out_shape=jax.ShapeDtypeStruct(potential.shape, f32),
        in_specs=[SMEM] * 3 + [VMEM] * 3,
        out_specs=VMEM,
        name="place",
    )(positions, before, after, terms, from_before, from_after)


def solution(mesh):
    in_specs = (P("depth", "probe", None), P(), P("probe", None), P("probe", None, None))
    out_specs = P("depth", "probe", None)
    return jax.shard_map(local, mesh=mesh, in_specs=in_specs, out_specs=out_specs, check_vma=False)
```

```python
import functools

import jax
import jax.numpy as jnp
import numpy as np
from jax import lax
from jax.experimental import pallas as pl
from jax.experimental.pallas import tpu as pltpu
from jax.sharding import PartitionSpec as P

interaction = 0.5
fresnel_phase = 60.0
f32 = jnp.float32
bf16 = jnp.bfloat16

VMEM = pl.BlockSpec(memory_space=pltpu.VMEM)
SMEM = pl.BlockSpec(memory_space=pltpu.SMEM)
ANY = pl.BlockSpec(memory_space=pl.ANY)


def poly_tables():
    x = np.cos(np.linspace(0.0, np.pi / 2, 4001)) * (np.pi / 2) * 1.0005
    z = x * x
    fit = np.polynomial.chebyshev.Chebyshev.fit
    kind = np.polynomial.Polynomial
    sine = fit(z, np.sinc(x / np.pi), 5).convert(kind=kind).coef
    cosine = fit(z, np.cos(x), 5).convert(kind=kind).coef
    return [float(v) for v in sine], [float(v) for v in cosine]


def split_table(matrix):
    parts = []
    for real in (matrix.real, matrix.imag, -matrix.imag):
        wide = real.astype(np.float32)
        high = wide.astype(bf16)
        parts.append(high)
        parts.append((real - high.astype(np.float64)).astype(np.float32).astype(bf16))
    return np.stack(parts)


def tables(extent):
    index = np.arange(extent)
    dft = np.exp(-2j * np.pi * ((index[:, None] * index[None, :]) % extent) / extent)
    dft = dft / np.sqrt(extent)
    frequency = ((index + extent // 2) % extent - extent // 2) / extent
    chirp = np.exp(-1j * fresnel_phase * frequency**2)
    propagator = np.conj(dft) @ (chirp[:, None] * dft)
    return split_table(propagator), split_table(dft)


def sin_cos(window):
    sine, cosine = poly_tables()
    half = window * (interaction / 2)
    turns = jnp.round(half * (1.0 / np.pi))
    pi_high = float(np.float32(3.140625))
    pi_low = float(np.pi - 3.140625)
    x = (half - turns * pi_high) - turns * pi_low
    z = x * x
    s = sine[5]
    c = cosine[5]
    for k in range(4, -1, -1):
        s = s * z + sine[k]
        c = c * z + cosine[k]
    s = s * x
    return 2.0 * s * c, 1.0 - 2.0 * (s * s)


def parts_of(x):
    high = x.astype(bf16)
    return high, (x - high.astype(f32)).astype(bf16)


def dot(a, b):
    return jnp.dot(a, b, preferred_element_type=f32)


def sandwich(m, real, imag):
    m = [m[k] for k in range(6)]
    rows = jnp.concatenate
    rh, rl = parts_of(real)
    ih, il = parts_of(imag)
    left = rows([rh, rl, rh, ih, il, ih], axis=1)
    yr = dot(left, rows([m[0], m[0], m[1], m[4], m[4], m[5]], axis=0))
    yi = dot(left, rows([m[2], m[2], m[3], m[0], m[0], m[1]], axis=0))
    rh, rl = parts_of(yr)
    ih, il = parts_of(yi)
    right = rows([rh, rl, rh, ih, il, ih], axis=0)
    zr = dot(rows([m[0], m[0], m[1], m[4], m[4], m[5]], axis=1), right)
    zi = dot(rows([m[2], m[2], m[3], m[0], m[0], m[1]], axis=1), right)
    return zr, zi


def call(kernel, name, results, scalars, arrays, scratch=(), limit=16):
    arrays = [pltpu.with_memory_space_constraint(x, pltpu.VMEM) for x in arrays]
    out = pl.pallas_call(
        kernel,
        out_shape=[pltpu.VMEM(shape, f32) for shape in results],
        in_specs=[SMEM] * len(scalars) + [VMEM] * len(arrays),
        out_specs=[VMEM] * len(results),
        scratch_shapes=list(scratch),
        compiler_params=pltpu.CompilerParams(vmem_limit_bytes=limit * 2**20),
        name=name,
    )(*scalars, *arrays)
    return out


def entry(position, k):
    return position[0:1, k : k + 1]


def covered(column, block, shape):
    lane = lax.broadcasted_iota(jnp.int32, shape, 1) + block * shape[1]
    return (lane >= column) & (lane < column + shape[1])


def cut_kernel(*refs):
    count = (len(refs) - 1) // 2
    potential = refs[count]
    layers, strip, columns = potential.shape
    extent = 2 * strip
    for k in range(count):
        out = refs[count + 1 + k]
        column = entry(refs[k], 1)
        for layer in range(layers):
            value = potential[layer, :, :extent]
            for block in range(1, columns // extent):
                mask = covered(column, block, value.shape)
                next_value = potential[layer, :, block * extent : (block + 1) * extent]
                value = jnp.where(mask, next_value, value)
            out[layer] = value


def cut(potential, *positions):
    layers, strip, _ = potential.shape
    shapes = [(layers, strip, 2 * strip)] * len(positions)
    return call(cut_kernel, "cut", shapes, [], [*positions, potential])


def prepare_kernel(*refs):
    count = len(refs) // 2
    for k in range(count):
        for layer in range(refs[k].shape[0]):
            s, c = sin_cos(refs[k][layer])
            refs[count + k][layer, 0] = c
            refs[count + k][layer, 1] = s


def prepare(*pieces):
    shapes = [(x.shape[0], 2, *x.shape[1:]) for x in pieces]
    return call(prepare_kernel, "prepare", shapes, [], pieces)


def merge_kernel(position, above, below, out):
    layers, strip, extent = out.shape
    row = lax.broadcasted_iota(jnp.int32, (strip, extent), 0)
    mask = row >= entry(position, 0) % strip
    for layer in range(layers):
        out[layer] = jnp.where(mask, above[layer], below[layer])


def transmit(trans, real, imag):
    c, s = trans
    return c * real - s * imag, c * imag + s * real


def joined(upper, lower, layer):
    return [jnp.concatenate([upper[layer, k], lower[layer, k]], axis=0) for k in range(2)]


def enter_kernel(place, position, probe, prop, upper, other, wave_out, saved, lower):
    layers, strip, extent = other.shape
    for layer in range(layers):
        s, c = sin_cos(other[layer])
        lower[layer, 0] = c
        lower[layer, 1] = s
    row_shift = position[0, 0] % strip + strip
    column_shift = position[0, 1] % extent
    for k in range(2):
        wave_out[k] = pltpu.roll(pltpu.roll(probe[k], row_shift, 0), column_shift, 1)

    def forward(layer, wave):
        wave = transmit(joined(upper, lower, layer), *wave)
        saved[layer, 0] = wave[0]
        saved[layer, 1] = wave[1]
        return sandwich(prop, *wave)

    @pl.when(place[0] == 0)
    def _():
        wave = lax.fori_loop(0, layers, forward, (wave_out[0], wave_out[1]))
        wave_out[0] = wave[0]
        wave_out[1] = wave[1]


def solve_kernel(count, place, wave_in, saved_in, intensity, prop, dft, *refs):
    uppers = refs[:count]
    lower = refs[count]
    others = refs[count + 1 : 2 * count]
    mine, other, trans, saved = refs[2 * count :]
    layers, strip, extent = mine.shape
    slices = layers * count
    depth = place[0]
    for k in range(count):
        owner = (depth - k + count) % count
        for layer in range(layers):
            if k == 0:
                half = lower[layer, 0], lower[layer, 1]
            else:
                half = sin_cos(others[k - 1][layer])[::-1]
            for part in range(2):
                trans[owner * layers + layer, part, :strip] = uppers[k][layer, part]
                trans[owner * layers + layer, part, strip:] = half[part]

    @pl.when(depth == 0)
    def _():
        for layer in range(layers):
            for part in range(2):
                saved[layer, part] = saved_in[layer, part]

    def forward(s, wave):
        wave = transmit((trans[s, 0], trans[s, 1]), *wave)
        saved[s, 0] = wave[0]
        saved[s, 1] = wave[1]
        return sandwich(prop, *wave)

    wave = (wave_in[0], wave_in[1])
    wave = lax.fori_loop(jnp.where(depth == 0, layers, 0), slices - 1, forward, wave)
    last = slices - 1
    real, imag = transmit((trans[last, 0], trans[last, 1]), *wave)
    saved[last, 0] = real
    saved[last, 1] = imag
    far_real, far_imag = sandwich(dft, real, imag)
    misfit = far_real * far_real + far_imag * far_imag - intensity[0]
    wave = sandwich(dft, misfit * far_real, -(misfit * far_imag))

    def term(s, wave):
        @pl.when(s < (depth + 1) * layers)
        def _():
            value = -interaction * (wave[1] * saved[s, 0] + wave[0] * saved[s, 1])
            mine[s - depth * layers] = value[:strip]
            other[s - depth * layers] = value[strip:]

    term(last, wave)

    def backward(step, wave):
        s = last - step
        wave = sandwich(prop, *transmit((trans[s, 0], trans[s, 1]), *wave))
        term(s - 1, wave)
        return wave

    lax.fori_loop(0, last - depth * layers, backward, wave)


def place_kernel(position, before, after, own, from_before, from_after, out, staged, sems):
    layers, strip, columns = out.shape
    extent = 2 * strip
    shape = (strip, extent)
    row = lax.broadcasted_iota(jnp.int32, shape, 0)
    below = row < entry(before, 0) % strip
    above = row >= entry(after, 0) % strip
    copies = []
    for block in range(columns // extent):
        at = slice(block * extent, (block + 1) * extent)
        mine = covered(entry(position, 1), block, shape)
        low = covered(entry(before, 1), block, shape) & below
        high = covered(entry(after, 1), block, shape) & above
        for layer in range(layers):
            value = jnp.where(mine, own[layer], 0.0)
            value = value + jnp.where(low, from_before[layer], 0.0)
            value = value + jnp.where(high, from_after[layer], 0.0)
            staged[layer, :, at] = value
        copy = pltpu.make_async_copy(staged.at[:, :, at], out.at[:, :, at], sems.at[block])
        copy.start()
        copies.append(copy)
    for copy in copies:
        copy.wait()


def local(potential, probe, positions, intensity):
    layers, strip, columns = potential.shape
    extent = probe.shape[1]
    assert positions.shape[0] == 1 and extent == 2 * strip and columns % extent == 0
    count = lax.axis_size("probe")
    depth_count = lax.axis_size("depth")
    slices = layers * depth_count
    onward = [(i, (i + 1) % count) for i in range(count)]
    backward = [(i, (i - 1) % count) for i in range(count)]
    before = lax.ppermute(positions, "probe", onward)
    after = lax.ppermute(positions, "probe", backward)

    def from_depths(x):
        out = [x]
        for k in range(1, depth_count):
            pairs = [(i, (i + k) % depth_count) for i in range(depth_count)]
            out.append(lax.ppermute(x, "depth", pairs))
        return out

    (own,) = cut(potential, positions)
    owns = from_depths(own)
    for_after, for_before = cut(potential, after, before)
    above = lax.ppermute(for_after, "probe", onward)
    below = lax.ppermute(for_before, "probe", backward)
    uppers = [prepare(x)[0] for x in owns]
    half = (layers, strip, extent)
    (other,) = call(merge_kernel, "merge", [half], [], [positions, above, below])
    others = from_depths(other)
    place = lax.axis_index("depth").astype(jnp.int32).reshape(1)
    prop, dft = [jnp.asarray(x) for x in tables(extent)]
    field = (2, extent, extent)
    wave, saved, lower = call(
        enter_kernel,
        "enter",
        [field, (layers, *field), (layers, 2, strip, extent)],
        [place, positions],
        [probe, prop, uppers[0], other],
    )
    mine, outer = call(
        functools.partial(solve_kernel, depth_count),
        "solve",
        [half, half],
        [place],
        [wave, saved, intensity, prop, dft, *uppers, lower, *others[1:]],
        scratch=[pltpu.VMEM((slices, *field), f32)] * 2,
        limit=12 + slices * 4 * extent * extent // 2**20 * 4 + 8,
    )
    from_before = lax.ppermute(outer, "probe", onward)
    from_after = lax.ppermute(outer, "probe", backward)
    arrays = [positions, before, after, mine, from_before, from_after]
    arrays = [pltpu.with_memory_space_constraint(x, pltpu.VMEM) for x in arrays]
    return pl.pallas_call(
        place_kernel,
        out_shape=jax.ShapeDtypeStruct(potential.shape, f32),
        in_specs=[VMEM] * 6,
        out_specs=ANY,
        scratch_shapes=[
            pltpu.VMEM(potential.shape, f32),
            pltpu.SemaphoreType.DMA((columns // extent,)),
        ],
        name="place",
    )(*arrays)


def solution(mesh):
    in_specs = (P("depth", "probe", None), P(), P("probe", None), P("probe", None, None))
    out_specs = P("depth", "probe", None)
    return jax.shard_map(local, mesh=mesh, in_specs=in_specs, out_specs=out_specs, check_vma=False)
```

```python
import functools

import jax
import jax.numpy as jnp
import numpy as np
from jax import lax
from jax.experimental import pallas as pl
from jax.experimental.pallas import tpu as pltpu
from jax.sharding import PartitionSpec as P

interaction = 0.5
fresnel_phase = 60.0
f32 = jnp.float32
bf16 = jnp.bfloat16

VMEM = pl.BlockSpec(memory_space=pltpu.VMEM)
SMEM = pl.BlockSpec(memory_space=pltpu.SMEM)
ANY = pl.BlockSpec(memory_space=pl.ANY)


def poly_tables():
    x = np.cos(np.linspace(0.0, np.pi / 2, 4001)) * (np.pi / 2) * 1.0005
    z = x * x
    fit = np.polynomial.chebyshev.Chebyshev.fit
    kind = np.polynomial.Polynomial
    sine = fit(z, np.sinc(x / np.pi), 5).convert(kind=kind).coef
    cosine = fit(z, np.cos(x), 5).convert(kind=kind).coef
    return [float(v) for v in sine], [float(v) for v in cosine]


def split_table(matrix):
    parts = []
    for real in (matrix.real, matrix.imag, -matrix.imag):
        wide = real.astype(np.float32)
        high = wide.astype(bf16)
        parts.append(high)
        parts.append((real - high.astype(np.float64)).astype(np.float32).astype(bf16))
    return np.stack(parts)


def tables(extent):
    index = np.arange(extent)
    dft = np.exp(-2j * np.pi * ((index[:, None] * index[None, :]) % extent) / extent)
    dft = dft / np.sqrt(extent)
    frequency = ((index + extent // 2) % extent - extent // 2) / extent
    chirp = np.exp(-1j * fresnel_phase * frequency**2)
    propagator = np.conj(dft) @ (chirp[:, None] * dft)
    return split_table(propagator), split_table(dft)


def sin_cos(window):
    sine, cosine = poly_tables()
    half = window * (interaction / 2)
    turns = jnp.round(half * (1.0 / np.pi))
    pi_high = float(np.float32(3.140625))
    pi_low = float(np.pi - 3.140625)
    x = (half - turns * pi_high) - turns * pi_low
    z = x * x
    s = sine[5]
    c = cosine[5]
    for k in range(4, -1, -1):
        s = s * z + sine[k]
        c = c * z + cosine[k]
    s = s * x
    return 2.0 * s * c, 1.0 - 2.0 * (s * s)


def parts_of(x):
    high = x.astype(bf16)
    return high, (x - high.astype(f32)).astype(bf16)


def dot(a, b):
    return jnp.dot(a, b, preferred_element_type=f32)


def sandwich(m, real, imag):
    m = [m[k] for k in range(6)]
    rows = jnp.concatenate
    rh, rl = parts_of(real)
    ih, il = parts_of(imag)
    left = rows([rh, rl, rh, ih, il, ih], axis=1)
    yr = dot(left, rows([m[0], m[0], m[1], m[4], m[4], m[5]], axis=0))
    yi = dot(left, rows([m[2], m[2], m[3], m[0], m[0], m[1]], axis=0))
    rh, rl = parts_of(yr)
    ih, il = parts_of(yi)
    right = rows([rh, rl, rh, ih, il, ih], axis=0)
    zr = dot(rows([m[0], m[0], m[1], m[4], m[4], m[5]], axis=1), right)
    zi = dot(rows([m[2], m[2], m[3], m[0], m[0], m[1]], axis=1), right)
    return zr, zi


def call(kernel, name, results, scalars, arrays, aliases=(), scratch=(), limit=16):
    arrays = [pltpu.with_memory_space_constraint(x, pltpu.VMEM) for x in arrays]
    return pl.pallas_call(
        kernel,
        out_shape=[pltpu.VMEM(shape, f32) for shape in results],
        in_specs=[SMEM] * len(scalars) + [VMEM] * len(arrays),
        out_specs=[VMEM] * len(results),
        input_output_aliases={len(scalars) + i: o for i, o in aliases},
        scratch_shapes=list(scratch),
        compiler_params=pltpu.CompilerParams(vmem_limit_bytes=limit * 2**20),
        name=name,
    )(*scalars, *arrays)


def entry(position, k):
    return position[0:1, k : k + 1]


def covered(column, block, shape):
    lane = lax.broadcasted_iota(jnp.int32, shape, 1) + block * shape[1]
    return (lane >= column) & (lane < column + shape[1])


def fold_columns(potential, position, out):
    layers, strip, columns = potential.shape
    extent = 2 * strip
    column = entry(position, 1)
    for layer in range(layers):
        value = potential[layer, :, :extent]
        for block in range(1, columns // extent):
            mask = covered(column, block, value.shape)
            next_value = potential[layer, :, block * extent : (block + 1) * extent]
            value = jnp.where(mask, next_value, value)
        out[layer] = value


def own_kernel(position, potential, tile, own, sem):
    copy = pltpu.make_async_copy(potential, tile, sem)
    copy.start()
    copy.wait()
    fold_columns(tile, position, own)


def cut_kernel(fast, slow, tile, for_fast, for_slow):
    fold_columns(tile, slow, for_slow)
    fold_columns(tile, fast, for_fast)


def fill(table, owner, piece, rows):
    layers = piece.shape[0]
    for layer in range(layers):
        s, c = sin_cos(piece[layer])
        table[owner * layers + layer, 0, rows] = c
        table[owner * layers + layer, 1, rows] = s


def first_kernel(place, position, own, probe, table, wave):
    strip = own.shape[1]
    row_shift = position[0, 0] % strip + strip
    column_shift = position[0, 1] % (2 * strip)
    for k in range(2):
        wave[k] = pltpu.roll(pltpu.roll(probe[k], row_shift, 0), column_shift, 1)
    fill(table, place[0], own, slice(0, strip))


def second_kernel(count, place, *refs):
    owns, table = refs[: count - 1], refs[-1]
    strip = owns[0].shape[1]
    for k in range(1, count):
        fill(table, (place[0] - k + count) % count, owns[k - 1], slice(0, strip))


def merge_kernel(parity, position, fast, slow, _, out):
    layers, strip, extent = out.shape
    row = lax.broadcasted_iota(jnp.int32, (strip, extent), 0)
    above = (row >= entry(position, 0) % strip).astype(jnp.int32)
    mask = above != parity[0]
    for layer in range(layers):
        out[layer] = jnp.where(mask, slow[layer], fast[layer])


def transmit(trans, real, imag):
    c, s = trans
    return c * real - s * imag, c * imag + s * real


def enter_kernel(place, wave_in, other, prop, table_in, wave_out, table, saved):
    layers, strip, _ = other.shape
    fill(table, place[0], other, slice(strip, 2 * strip))

    def forward(layer, wave):
        wave = transmit((table[layer, 0], table[layer, 1]), *wave)
        saved[layer, 0] = wave[0]
        saved[layer, 1] = wave[1]
        return sandwich(prop, *wave)

    @pl.when(place[0] == 0)
    def _():
        wave = lax.fori_loop(0, layers, forward, (wave_in[0], wave_in[1]))
        wave_out[0] = wave[0]
        wave_out[1] = wave[1]


def solve_kernel(count, place, wave_in, saved_in, intensity, prop, dft, table_in, *refs):
    others = refs[: count - 1]
    mine, outer, table, saved = refs[count - 1 :]
    layers, strip, extent = mine.shape
    slices = layers * count
    last = slices - 1
    depth = place[0]
    first = depth * layers
    for k in range(1, count):
        fill(table, (depth - k + count) % count, others[k - 1], slice(strip, extent))

    def enter(s, wave):
        wave = transmit((table[s, 0], table[s, 1]), *wave)

        @pl.when((s >= first) & (s < first + layers))
        def _():
            saved[s - first, 0] = wave[0]
            saved[s - first, 1] = wave[1]

        return wave

    wave = (wave_in[0], wave_in[1])
    start = jnp.where(depth == 0, layers, 0)
    wave = lax.fori_loop(start, last, lambda s, w: sandwich(prop, *enter(s, w)), wave)
    far_real, far_imag = sandwich(dft, *enter(last, wave))
    misfit = far_real * far_real + far_imag * far_imag - intensity[0]
    wave = sandwich(dft, misfit * far_real, -(misfit * far_imag))

    def term(s, wave):
        @pl.when(s < first + layers)
        def _():
            value = wave[1] * saved[s - first, 0] + wave[0] * saved[s - first, 1]
            value = -interaction * value
            mine[s - first] = value[:strip]
            outer[s - first] = value[strip:]

    term(last, wave)

    def backward(step, wave):
        s = last - step
        wave = sandwich(prop, *transmit((table[s, 0], table[s, 1]), *wave))
        term(s - 1, wave)
        return wave

    lax.fori_loop(0, last - first, backward, wave)


def covers(position, block, shape, odd):
    strip = shape[0]
    row = lax.broadcasted_iota(jnp.int32, shape, 0)
    rows = (row >= entry(position, 0) % strip).astype(jnp.int32) != odd
    return covered(entry(position, 1), block, shape) & rows


def stage_kernel(parity, position, fast_position, mine, fast, staged):
    layers, strip, columns = staged.shape
    extent = 2 * strip
    shape = (strip, extent)
    for block in range(columns // extent):
        at = slice(block * extent, (block + 1) * extent)
        own = covered(entry(position, 1), block, shape)
        near = covers(fast_position, block, shape, parity[0])
        for layer in range(layers):
            value = jnp.where(own, mine[layer], 0.0) + jnp.where(near, fast[layer], 0.0)
            staged[layer, :, at] = value


def place_kernel(parity, slow_position, slow, staged, out, final, sems):
    layers, strip, columns = out.shape
    extent = 2 * strip
    copies = []
    for block in range(columns // extent):
        at = slice(block * extent, (block + 1) * extent)
        far = covers(slow_position, block, (strip, extent), 1 - parity[0])
        for layer in range(layers):
            value = staged[layer, :, at] + jnp.where(far, slow[layer], 0.0)
            final[layer, :, at] = value
        copy = pltpu.make_async_copy(final.at[:, :, at], out.at[:, :, at], sems.at[block])
        copy.start()
        copies.append(copy)
    for copy in copies:
        copy.wait()


def local(potential, probe, positions, intensity):
    layers, strip, columns = potential.shape
    extent = probe.shape[1]
    count = lax.axis_size("probe")
    depth_count = lax.axis_size("depth")
    assert positions.shape[0] == 1 and extent == 2 * strip and columns % extent == 0
    assert count % 2 == 0
    slices = layers * depth_count
    half = (layers, strip, extent)
    field = (2, extent, extent)
    fast_pairs = [(i, i ^ 1) for i in range(count)]
    slow_pairs = [(i, (i + 1 if i % 2 else i - 1) % count) for i in range(count)]

    def swapped(fast, slow):
        slow = lax.ppermute(slow, "probe", slow_pairs)
        return lax.ppermute(fast, "probe", fast_pairs), slow

    def from_depths(x):
        out = []
        for k in range(1, depth_count):
            pairs = [(i, (i + k) % depth_count) for i in range(depth_count)]
            out.append(lax.ppermute(x, "depth", pairs))
        return out

    place = lax.axis_index("depth").astype(jnp.int32).reshape(1)
    parity = (lax.axis_index("probe").astype(jnp.int32) % 2).reshape(1)
    prop, dft = [jnp.asarray(x) for x in tables(extent)]

    fast_position, slow_position = swapped(positions, positions)
    tile, own = pl.pallas_call(
        own_kernel,
        out_shape=[pltpu.VMEM(potential.shape, f32), pltpu.VMEM(half, f32)],
        in_specs=[VMEM, ANY],
        out_specs=[VMEM] * 2,
        scratch_shapes=[pltpu.SemaphoreType.DMA],
        name="own",
    )(positions, potential)
    owns = from_depths(own)
    pieces = call(cut_kernel, "cut", [half] * 2, [], [fast_position, slow_position, tile])
    fast, slow = swapped(*pieces)
    table, wave = call(
        first_kernel, "first", [(slices, *field), field], [place, positions], [own, probe]
    )
    (table,) = call(
        functools.partial(second_kernel, depth_count),
        "second",
        [table.shape],
        [place],
        [*owns, table],
        aliases=[(depth_count - 1, 0)],
    )
    (other,) = call(merge_kernel, "merge", [half], [parity], [positions, fast, slow, table])
    others = from_depths(other)
    wave, table, saved = call(
        enter_kernel,
        "enter",
        [field, table.shape, (layers, *field)],
        [place],
        [wave, other, prop, table],
        aliases=[(0, 0), (3, 1)],
    )
    mine, outer, _, _ = call(
        functools.partial(solve_kernel, depth_count),
        "solve",
        [half, half, table.shape, saved.shape],
        [place],
        [wave, saved, intensity, prop, dft, table, *others],
        aliases=[(5, 2), (1, 3)],
    )
    fast, slow = swapped(outer, outer)
    (staged,) = call(
        stage_kernel, "stage", [potential.shape], [parity], [positions, fast_position, mine, fast]
    )
    arrays = [slow_position, slow, staged]
    arrays = [pltpu.with_memory_space_constraint(x, pltpu.VMEM) for x in arrays]
    return pl.pallas_call(
        place_kernel,
        out_shape=jax.ShapeDtypeStruct(potential.shape, f32),
        in_specs=[SMEM] + [VMEM] * 3,
        out_specs=ANY,
        scratch_shapes=[
            pltpu.VMEM(potential.shape, f32),
            pltpu.SemaphoreType.DMA((columns // extent,)),
        ],
        name="place",
    )(parity, *arrays)


def solution(mesh):
    in_specs = (P("depth", "probe", None), P(), P("probe", None), P("probe", None, None))
    out_specs = P("depth", "probe", None)
    return jax.shard_map(local, mesh=mesh, in_specs=in_specs, out_specs=out_specs, check_vma=False)
```

```python
import functools

import jax
import jax.numpy as jnp
import numpy as np
from jax import lax
from jax.experimental import pallas as pl
from jax.experimental.pallas import tpu as pltpu
from jax.sharding import PartitionSpec as P

interaction = 0.5
fresnel_phase = 60.0
f32 = jnp.float32
bf16 = jnp.bfloat16

VMEM = pl.BlockSpec(memory_space=pltpu.VMEM)
SMEM = pl.BlockSpec(memory_space=pltpu.SMEM)
ANY = pl.BlockSpec(memory_space=pl.ANY)


def poly_tables():
    x = np.cos(np.linspace(0.0, np.pi / 2, 4001)) * (np.pi / 2) * 1.0005
    z = x * x
    fit = np.polynomial.chebyshev.Chebyshev.fit
    kind = np.polynomial.Polynomial
    sine = fit(z, np.sinc(x / np.pi), 5).convert(kind=kind).coef
    cosine = fit(z, np.cos(x), 5).convert(kind=kind).coef
    return [float(v) for v in sine], [float(v) for v in cosine]


def split_table(matrix):
    parts = []
    for real in (matrix.real, matrix.imag, -matrix.imag):
        wide = real.astype(np.float32)
        high = wide.astype(bf16)
        parts.append(high)
        parts.append((real - high.astype(np.float64)).astype(np.float32).astype(bf16))
    return np.stack(parts)


def tables(extent):
    index = np.arange(extent)
    dft = np.exp(-2j * np.pi * ((index[:, None] * index[None, :]) % extent) / extent)
    dft = dft / np.sqrt(extent)
    frequency = ((index + extent // 2) % extent - extent // 2) / extent
    chirp = np.exp(-1j * fresnel_phase * frequency**2)
    propagator = np.conj(dft) @ (chirp[:, None] * dft)
    return split_table(propagator), split_table(dft)


def sin_cos(window):
    sine, cosine = poly_tables()
    half = window * (interaction / 2)
    turns = jnp.round(half * (1.0 / np.pi))
    pi_high = float(np.float32(3.140625))
    pi_low = float(np.pi - 3.140625)
    x = (half - turns * pi_high) - turns * pi_low
    z = x * x
    s = sine[5]
    c = cosine[5]
    for k in range(4, -1, -1):
        s = s * z + sine[k]
        c = c * z + cosine[k]
    s = s * x
    return 2.0 * s * c, 1.0 - 2.0 * (s * s)


def parts_of(x):
    high = x.astype(bf16)
    return high, (x - high.astype(f32)).astype(bf16)


def dot(a, b):
    return jnp.dot(a, b, preferred_element_type=f32)


def sandwich(m, real, imag):
    m = [m[k] for k in range(6)]
    rows = jnp.concatenate
    rh, rl = parts_of(real)
    ih, il = parts_of(imag)
    left = rows([rh, rl, rh, ih, il, ih], axis=1)
    yr = dot(left, rows([m[0], m[0], m[1], m[4], m[4], m[5]], axis=0))
    yi = dot(left, rows([m[2], m[2], m[3], m[0], m[0], m[1]], axis=0))
    rh, rl = parts_of(yr)
    ih, il = parts_of(yi)
    right = rows([rh, rl, rh, ih, il, ih], axis=0)
    zr = dot(rows([m[0], m[0], m[1], m[4], m[4], m[5]], axis=1), right)
    zi = dot(rows([m[2], m[2], m[3], m[0], m[0], m[1]], axis=1), right)
    return zr, zi


def call(kernel, results, scalars, arrays, aliases=(), scratch=(), limit=6):
    arrays = [pltpu.with_memory_space_constraint(x, pltpu.VMEM) for x in arrays]
    return pl.pallas_call(
        kernel,
        out_shape=[pltpu.VMEM(shape, f32) for shape in results],
        in_specs=[SMEM] * len(scalars) + [VMEM] * len(arrays),
        out_specs=[VMEM] * len(results),
        input_output_aliases={len(scalars) + i: o for i, o in aliases},
        scratch_shapes=list(scratch),
        compiler_params=pltpu.CompilerParams(vmem_limit_bytes=limit * 2**20),
    )(*scalars, *arrays)


def entry(position, k):
    return position[0:1, k : k + 1]


def covered(column, block, shape):
    lane = lax.broadcasted_iota(jnp.int32, shape, 1) + block * shape[1]
    return (lane >= column) & (lane < column + shape[1])


def fold_columns(potential, position, out):
    layers, strip, columns = potential.shape
    extent = 2 * strip
    column = entry(position, 1)
    for layer in range(layers):
        value = potential[layer, :, :extent]
        for block in range(1, columns // extent):
            mask = covered(column, block, value.shape)
            next_value = potential[layer, :, block * extent : (block + 1) * extent]
            value = jnp.where(mask, next_value, value)
        out[layer] = value


def tile_kernel(potential, tile, sems):
    layers, strip, _ = potential.shape
    copies = []
    for k in range(8):
        at = (k // (8 // layers), slice(k % (8 // layers) * strip * layers // 8, (k % (8 // layers) + 1) * strip * layers // 8))
        copies.append(pltpu.make_async_copy(potential.at[at], tile.at[at], sems.at[k]))
        copies[k].start()
    for copy in copies:
        copy.wait()


def cut_kernel(position, tile, *refs):
    fold_columns(tile, position, refs[-1])


def fill(table, slices, rows, piece):
    for layer, at in enumerate(slices):
        s, c = sin_cos(piece(layer))
        table[at, 0, rows] = c
        table[at, 1, rows] = s


def slices_of(depth, k, count, layers):
    first = (depth - k + count) % count * layers
    return [first + layer for layer in range(layers)]


def outside(position, above, below):
    row = lax.broadcasted_iota(jnp.int32, above.shape[1:], 0)
    mask = row >= entry(position, 0) % above.shape[1]
    return lambda layer: jnp.where(mask, above[layer], below[layer])


def first_kernel(place, position, own, probe, prop, dft, table, wave):
    strip = own.shape[1]
    row_shift = position[0, 0] % strip + strip
    column_shift = position[0, 1] % (2 * strip)
    for k in range(2):
        wave[k] = pltpu.roll(pltpu.roll(probe[k], row_shift, 0), column_shift, 1)
    layers = own.shape[0]
    slices = [place[0] * layers + layer for layer in range(layers)]
    fill(table, slices, slice(0, strip), lambda layer: own[layer])


def merge_kernel(position, above, below, _, *out):
    piece = outside(position, above, below)
    for layer in range(above.shape[0]):
        out[layer][...] = piece(layer)


def transmit(trans, real, imag):
    c, s = trans
    return c * real - s * imag, c * imag + s * real


def enter_kernel(layers, place, wave_in, prop, table_in, *refs):
    others = refs[:layers]
    wave_out, table, saved = refs[layers:]
    strip, extent = others[0].shape
    slices = [place[0] * layers + layer for layer in range(layers)]
    fill(table, slices, slice(strip, extent), lambda layer: others[layer][...])

    def forward(layer, wave):
        wave = transmit((table[layer, 0], table[layer, 1]), *wave)
        saved[layer, 0] = wave[0]
        saved[layer, 1] = wave[1]
        return sandwich(prop, *wave)

    @pl.when(place[0] == 0)
    def _():
        wave = lax.fori_loop(0, layers, forward, (wave_in[0], wave_in[1]))
        wave_out[0] = wave[0]
        wave_out[1] = wave[1]


def middle_kernel(count, layers, place, wave_in, prop, table_in, *refs):
    owns = refs[: count - 1]
    others = refs[count - 1 : 2 * count - 2]
    wave_out, table = refs[2 * count - 2 :]
    strip, extent = others[0].shape
    owners = [slices_of(place[0], k, count, layers)[0] for k in range(1, count)]
    fill(table, owners, slice(0, strip), lambda k: owns[k][0])
    fill(table, owners, slice(strip, extent), lambda k: others[k][...])
    s = jnp.where(place[0] == 0, layers, 0)
    wave = transmit((table[s, 0], table[s, 1]), wave_in[0], wave_in[1])
    wave_out[0], wave_out[1] = sandwich(prop, *wave)


def solve_kernel(count, place, wave_in, saved_in, intensity, prop, dft, table_in, *refs):
    mine, outer, table, saved = refs[-4:]
    layers, strip, extent = mine.shape
    slices = layers * count
    last = slices - 1
    depth = place[0]
    first = depth * layers
    for k in range(1, count):
        own = refs[k - 1]
        others = refs[count - 1 + (k - 1) * (layers - 1) : count - 1 + k * (layers - 1)]
        owners = slices_of(depth, k, count, layers)[1:]
        fill(table, owners, slice(0, strip), lambda layer: own[layer + 1])
        fill(table, owners, slice(strip, extent), lambda layer: others[layer][...])

    def enter(s, wave):
        wave = transmit((table[s, 0], table[s, 1]), *wave)

        @pl.when((s >= first) & (s < first + layers))
        def _():
            saved[s - first, 0] = wave[0]
            saved[s - first, 1] = wave[1]

        return wave

    wave = (wave_in[0], wave_in[1])
    start = jnp.where(depth == 0, layers + 1, 1)
    wave = lax.fori_loop(start, last, lambda s, w: sandwich(prop, *enter(s, w)), wave)
    far_real, far_imag = sandwich(dft, *enter(last, wave))
    misfit = far_real * far_real + far_imag * far_imag - intensity[0]
    wave = sandwich(dft, misfit * far_real, -(misfit * far_imag))

    def term(s, wave):
        @pl.when(s < first + layers)
        def _():
            value = wave[1] * saved[s - first, 0] + wave[0] * saved[s - first, 1]
            value = -interaction * value
            mine[s - first] = value[:strip]
            outer[s - first] = value[strip:]

    term(last, wave)

    def backward(step, wave):
        s = last - step
        wave = sandwich(prop, *transmit((table[s, 0], table[s, 1]), *wave))
        term(s - 1, wave)
        return wave

    lax.fori_loop(0, last - first, backward, wave)


def covers(position, block, shape, odd):
    strip = shape[0]
    row = lax.broadcasted_iota(jnp.int32, shape, 0)
    rows = (row >= entry(position, 0) % strip).astype(jnp.int32) != odd
    return covered(entry(position, 1), block, shape) & rows


def stage_kernel(parity, position, fast_position, mine, fast, staged):
    layers, strip, columns = staged.shape
    extent = 2 * strip
    shape = (strip, extent)
    for block in range(columns // extent):
        at = slice(block * extent, (block + 1) * extent)
        own = covered(entry(position, 1), block, shape)
        near = covers(fast_position, block, shape, parity[0])
        for layer in range(layers):
            value = jnp.where(own, mine[layer], 0.0) + jnp.where(near, fast[layer], 0.0)
            staged[layer, :, at] = value


def place_kernel(parity, slow_position, slow, staged, out, final, sems):
    layers, strip, columns = out.shape
    extent = 2 * strip
    copies = []
    for block in range(columns // extent):
        at = slice(block * extent, (block + 1) * extent)
        far = covers(slow_position, block, (strip, extent), 1 - parity[0])
        for layer in range(layers):
            value = staged[layer, :, at] + jnp.where(far, slow[layer], 0.0)
            final[layer, :, at] = value
        copy = pltpu.make_async_copy(final.at[:, :, at], out.at[:, :, at], sems.at[block])
        copy.start()
        copies.append(copy)
    for copy in copies:
        copy.wait()


def local(potential, probe, positions, intensity):
    layers, strip, columns = potential.shape
    extent = probe.shape[1]
    count = lax.axis_size("probe")
    depth_count = lax.axis_size("depth")
    assert positions.shape[0] == 1 and extent == 2 * strip and columns % extent == 0
    assert count % 2 == 0 and layers * (depth_count - 1) > 1
    slices = layers * depth_count
    half = (layers, strip, extent)
    field = (2, extent, extent)
    fast_pairs = [(i, i ^ 1) for i in range(count)]
    slow_pairs = [(i, (i + 1 if i % 2 else i - 1) % count) for i in range(count)]

    def swapped(fast, slow):
        slow = lax.ppermute(slow, "probe", slow_pairs)
        return lax.ppermute(fast, "probe", fast_pairs), slow

    def step(x, by):
        return lax.ppermute(x, "probe", [(i, (i + by) % count) for i in range(count)])

    def to_depths(x):
        out = []
        for k in range(1, depth_count):
            pairs = [(i, (i + k) % depth_count) for i in range(depth_count)]
            out.append(lax.ppermute(x, "depth", pairs))
        return out

    def cut(position, *after):
        return call(cut_kernel, [half], [], [position, tile, *after])[0]

    place = lax.axis_index("depth").astype(jnp.int32).reshape(1)
    parity = (lax.axis_index("probe").astype(jnp.int32) & 1).reshape(1)
    prop, dft = [jnp.asarray(x) for x in tables(extent)]

    before = step(positions, 1)
    after = step(positions, -1)
    (tile,) = pl.pallas_call(
        tile_kernel,
        out_shape=[pltpu.VMEM(potential.shape, f32)],
        in_specs=[ANY],
        out_specs=[VMEM],
        scratch_shapes=[pltpu.SemaphoreType.DMA((8,))],
        name="tile",
    )(potential)
    for_before = cut(before)
    below = step(for_before, -1)
    for_after = cut(after, for_before)
    above = step(for_after, 1)
    own = cut(positions, for_after)
    owns = to_depths(own)
    table, wave = call(
        first_kernel,
        [(slices, *field), field],
        [place, positions],
        [own, probe, prop, dft],
    )
    other = call(merge_kernel, [half[1:]] * layers, [], [positions, above, below, wave])
    others = []
    for layer in range(layers):
        others.append(to_depths(other[layer]))
    wave, table, saved = call(
        functools.partial(enter_kernel, layers),
        [field, table.shape, (layers, *field)],
        [place],
        [wave, prop, table, *other],
        aliases=[(0, 0), (2, 1)],
    )
    wave, table = call(
        functools.partial(middle_kernel, depth_count, layers),
        [field, table.shape],
        [place],
        [wave, prop, table, *owns, *others[0]],
        aliases=[(0, 0), (2, 1)],
    )
    rest = [others[layer][k] for k in range(depth_count - 1) for layer in range(1, layers)]
    mine, outer, _, _ = call(
        functools.partial(solve_kernel, depth_count),
        [half, half, table.shape, saved.shape],
        [place],
        [wave, saved, intensity, prop, dft, table, *owns, *rest],
        aliases=[(5, 2), (1, 3)],
    )
    odd = parity[0] == 1
    fast_position = jnp.where(odd, before, after)
    slow_position = jnp.where(odd, after, before)
    fast, slow = swapped(outer, outer)
    (staged,) = call(
        stage_kernel, [potential.shape], [parity], [positions, fast_position, mine, fast]
    )
    arrays = [slow_position, slow, staged]
    arrays = [pltpu.with_memory_space_constraint(x, pltpu.VMEM) for x in arrays]
    return pl.pallas_call(
        place_kernel,
        out_shape=jax.ShapeDtypeStruct(potential.shape, f32),
        in_specs=[SMEM] + [VMEM] * 3,
        out_specs=ANY,
        scratch_shapes=[
            pltpu.VMEM(potential.shape, f32),
            pltpu.SemaphoreType.DMA((columns // extent,)),
        ],
        name="place",
    )(parity, *arrays)


def solution(mesh):
    in_specs = (P("depth", "probe", None), P(), P("probe", None), P("probe", None, None))
    out_specs = P("depth", "probe", None)

    return jax.shard_map(
        local, mesh=mesh, in_specs=in_specs, out_specs=out_specs, check_vma=False
    )
```

```python
import functools

import jax
import jax.numpy as jnp
import numpy as np
from jax import lax
from jax.experimental import pallas as pl
from jax.experimental.pallas import tpu as pltpu
from jax.sharding import PartitionSpec as P

interaction = 0.5
fresnel_phase = 60.0
f32 = jnp.float32
bf16 = jnp.bfloat16

VMEM = pl.BlockSpec(memory_space=pltpu.VMEM)
SMEM = pl.BlockSpec(memory_space=pltpu.SMEM)
ANY = pl.BlockSpec(memory_space=pl.ANY)


def poly_tables():
    v = np.cos(np.linspace(0.0, np.pi / 2, 4001)) * 6.01
    h = interaction * v / 2
    fit = np.polynomial.chebyshev.Chebyshev.fit
    kind = np.polynomial.Polynomial
    sine = fit(v * v, interaction * np.sinc(h / np.pi), 4).convert(kind=kind).coef
    cosine = fit(v * v, np.cos(h), 5).convert(kind=kind).coef
    return [float(x) for x in sine], [float(x) for x in cosine]


def split_table(matrix):
    parts = []
    for real in (matrix.real, matrix.imag, -matrix.imag):
        wide = real.astype(np.float32)
        high = wide.astype(bf16)
        parts.append(high)
        parts.append((real - high.astype(np.float64)).astype(np.float32).astype(bf16))
    return np.stack(parts)


def tables(extent):
    index = np.arange(extent)
    dft = np.exp(-2j * np.pi * ((index[:, None] * index[None, :]) % extent) / extent)
    dft = dft / np.sqrt(extent)
    frequency = ((index + extent // 2) % extent - extent // 2) / extent
    chirp = np.exp(-1j * fresnel_phase * frequency**2)
    propagator = np.conj(dft) @ (chirp[:, None] * dft)
    return split_table(propagator), split_table(dft)


def sin_cos(window):
    sine, cosine = poly_tables()
    z = window * window
    s = sine[-1]
    for k in sine[-2::-1]:
        s = s * z + k
    s = s * window
    c = cosine[-1]
    for k in cosine[-2::-1]:
        c = c * z + k
    return s * c, 1.0 - (0.5 * s) * s


def parts_of(x):
    high = x.astype(bf16)
    return high, (x - high.astype(f32)).astype(bf16)


def dot(a, b):
    return jnp.dot(a, b, preferred_element_type=f32)


def sandwich(m, real, imag):
    m = [m[k] for k in range(6)]
    rows = jnp.concatenate
    rh, rl = parts_of(real)
    ih, il = parts_of(imag)
    left = rows([rh, rl, rh, ih, il, ih], axis=1)
    yr = dot(left, rows([m[0], m[0], m[1], m[4], m[4], m[5]], axis=0))
    yi = dot(left, rows([m[2], m[2], m[3], m[0], m[0], m[1]], axis=0))
    rh, rl = parts_of(yr)
    ih, il = parts_of(yi)
    right = rows([rh, rl, rh, ih, il, ih], axis=0)
    zr = dot(rows([m[0], m[0], m[1], m[4], m[4], m[5]], axis=1), right)
    zi = dot(rows([m[2], m[2], m[3], m[0], m[0], m[1]], axis=1), right)
    return zr, zi


def call(kernel, results, scalars, arrays, aliases=(), scratch=(), limit=4):
    arrays = [pltpu.with_memory_space_constraint(x, pltpu.VMEM) for x in arrays]
    return pl.pallas_call(
        kernel,
        out_shape=[pltpu.VMEM(shape, f32) for shape in results],
        in_specs=[SMEM] * len(scalars) + [VMEM] * len(arrays),
        out_specs=[VMEM] * len(results),
        input_output_aliases={len(scalars) + i: o for i, o in aliases},
        scratch_shapes=list(scratch),
        compiler_params=pltpu.CompilerParams(vmem_limit_bytes=limit * 2**20),
    )(*scalars, *arrays)


def entry(position, k):
    return position[0:1, k : k + 1]


def covered(column, block, shape):
    lane = lax.broadcasted_iota(jnp.int32, shape, 1) + block * shape[1]
    return (lane >= column) & (lane < column + shape[1])


def fold_columns(potential, position, out):
    layers, strip, columns = potential.shape
    extent = 2 * strip
    column = entry(position, 1)
    for layer in range(layers):
        value = potential[layer, :, :extent]
        for block in range(1, columns // extent):
            mask = covered(column, block, value.shape)
            next_value = potential[layer, :, block * extent : (block + 1) * extent]
            value = jnp.where(mask, next_value, value)
        out[layer] = value


def tile_kernel(potential, tile, sems):
    layers, strip, _ = potential.shape
    copies = []
    for k in range(8):
        at = (k // (8 // layers), slice(k % (8 // layers) * strip * layers // 8, (k % (8 // layers) + 1) * strip * layers // 8))
        copies.append(pltpu.make_async_copy(potential.at[at], tile.at[at], sems.at[k]))
        copies[k].start()
    for copy in copies:
        copy.wait()


def cut_kernel(position, tile, *refs):
    fold_columns(tile, position, refs[-1])


def fill(table, slices, rows, piece):
    for layer, at in enumerate(slices):
        s, c = sin_cos(piece(layer))
        table[at, 0, rows] = c
        table[at, 1, rows] = s


def slices_of(depth, k, count, layers):
    first = (depth - k + count) % count * layers
    return [first + layer for layer in range(layers)]


def outside(position, above, below):
    row = lax.broadcasted_iota(jnp.int32, above.shape[1:], 0)
    mask = row >= entry(position, 0) % above.shape[1]
    return lambda layer: jnp.where(mask, above[layer], below[layer])


def first_kernel(position, own, probe, _, upper, wave):
    layers, strip, _ = own.shape
    row_shift = position[0, 0] % strip + strip
    column_shift = position[0, 1] % (2 * strip)
    for k in range(2):
        wave[k] = pltpu.roll(pltpu.roll(probe[k], row_shift, 0), column_shift, 1)
    fill(upper, range(layers), slice(0, strip), lambda layer: own[layer])


def merge_kernel(position, above, below, _, *out):
    piece = outside(position, above, below)
    for layer in range(above.shape[0]):
        out[layer][...] = piece(layer)


def transmit(trans, real, imag):
    c, s = trans
    return c * real - s * imag, c * imag + s * real


def enter_kernel(layers, place, wave_in, prop, upper, *refs):
    others = refs[:layers]
    wave_out, table, saved = refs[layers:]
    strip, extent = others[0].shape
    slices = [place[0] * layers + layer for layer in range(layers)]
    for layer in range(layers):
        for part in range(2):
            table[slices[layer], part, :strip] = upper[layer, part]
    fill(table, slices, slice(strip, extent), lambda layer: others[layer][...])

    def forward(layer, wave):
        wave = transmit((table[layer, 0], table[layer, 1]), *wave)
        saved[layer, 0] = wave[0]
        saved[layer, 1] = wave[1]
        return sandwich(prop, *wave)

    @pl.when(place[0] == 0)
    def _():
        wave = lax.fori_loop(0, layers, forward, (wave_in[0], wave_in[1]))
        wave_out[0] = wave[0]
        wave_out[1] = wave[1]


def middle_kernel(count, layers, place, wave_in, prop, table_in, *refs):
    owns = refs[: count - 1]
    others = refs[count - 1 : 2 * count - 2]
    wave_out, table = refs[2 * count - 2 :]
    strip, extent = others[0].shape
    owners = [slices_of(place[0], k, count, layers)[0] for k in range(1, count)]
    fill(table, owners, slice(0, strip), lambda k: owns[k][0])
    fill(table, owners, slice(strip, extent), lambda k: others[k][...])
    s = jnp.where(place[0] == 0, layers, 0)
    wave = transmit((table[s, 0], table[s, 1]), wave_in[0], wave_in[1])
    wave_out[0], wave_out[1] = sandwich(prop, *wave)


def solve_kernel(count, place, wave_in, saved_in, intensity, prop, dft, table_in, *refs):
    mine, outer, table, saved = refs[-4:]
    layers, strip, extent = mine.shape
    slices = layers * count
    last = slices - 1
    depth = place[0]
    first = depth * layers
    for k in range(1, count):
        own = refs[k - 1]
        others = refs[count - 1 + (k - 1) * (layers - 1) : count - 1 + k * (layers - 1)]
        owners = slices_of(depth, k, count, layers)[1:]
        fill(table, owners, slice(0, strip), lambda layer: own[layer + 1])
        fill(table, owners, slice(strip, extent), lambda layer: others[layer][...])

    def enter(s, wave):
        wave = transmit((table[s, 0], table[s, 1]), *wave)

        @pl.when((s >= first) & (s < first + layers))
        def _():
            saved[s - first, 0] = wave[0]
            saved[s - first, 1] = wave[1]

        return wave

    wave = (wave_in[0], wave_in[1])
    start = jnp.where(depth == 0, layers + 1, 1)
    wave = lax.fori_loop(start, last, lambda s, w: sandwich(prop, *enter(s, w)), wave)
    far_real, far_imag = sandwich(dft, *enter(last, wave))
    misfit = far_real * far_real + far_imag * far_imag - intensity[0]
    wave = sandwich(dft, misfit * far_real, -(misfit * far_imag))

    def term(s, wave):
        @pl.when(s < first + layers)
        def _():
            value = wave[1] * saved[s - first, 0] + wave[0] * saved[s - first, 1]
            value = -interaction * value
            mine[s - first] = value[:strip]
            outer[s - first] = value[strip:]

    term(last, wave)

    def backward(step, wave):
        s = last - step
        wave = sandwich(prop, *transmit((table[s, 0], table[s, 1]), *wave))
        term(s - 1, wave)
        return wave

    lax.fori_loop(0, last - first, backward, wave)


def covers(position, block, shape, odd):
    strip = shape[0]
    row = lax.broadcasted_iota(jnp.int32, shape, 0)
    rows = (row >= entry(position, 0) % strip).astype(jnp.int32) != odd
    return covered(entry(position, 1), block, shape) & rows


def stage_kernel(parity, position, fast_position, mine, fast, staged):
    layers, strip, columns = staged.shape
    extent = 2 * strip
    shape = (strip, extent)
    for block in range(columns // extent):
        at = slice(block * extent, (block + 1) * extent)
        own = covered(entry(position, 1), block, shape)
        near = covers(fast_position, block, shape, parity[0])
        for layer in range(layers):
            value = jnp.where(own, mine[layer], 0.0) + jnp.where(near, fast[layer], 0.0)
            staged[layer, :, at] = value


def place_kernel(parity, slow_position, slow, staged, out, final, sems):
    layers, strip, columns = out.shape
    extent = 2 * strip
    copies = []
    for block in range(columns // extent):
        at = slice(block * extent, (block + 1) * extent)
        far = covers(slow_position, block, (strip, extent), 1 - parity[0])
        for layer in range(layers):
            value = staged[layer, :, at] + jnp.where(far, slow[layer], 0.0)
            final[layer, :, at] = value
        copy = pltpu.make_async_copy(final.at[:, :, at], out.at[:, :, at], sems.at[block])
        copy.start()
        copies.append(copy)
    for copy in copies:
        copy.wait()


def local(potential, probe, positions, intensity):
    layers, strip, columns = potential.shape
    extent = probe.shape[1]
    count = lax.axis_size("probe")
    depth_count = lax.axis_size("depth")
    assert positions.shape[0] == 1 and extent == 2 * strip and columns % extent == 0
    assert count % 2 == 0 and layers * (depth_count - 1) > 1
    slices = layers * depth_count
    half = (layers, strip, extent)
    field = (2, extent, extent)
    fast_pairs = [(i, i ^ 1) for i in range(count)]
    slow_pairs = [(i, (i + 1 if i % 2 else i - 1) % count) for i in range(count)]

    def swapped(fast, slow):
        slow = lax.ppermute(slow, "probe", slow_pairs)
        return lax.ppermute(fast, "probe", fast_pairs), slow

    def step(x, by):
        return lax.ppermute(x, "probe", [(i, (i + by) % count) for i in range(count)])

    def to_depths(x):
        out = []
        for k in range(1, depth_count):
            pairs = [(i, (i + k) % depth_count) for i in range(depth_count)]
            out.append(lax.ppermute(x, "depth", pairs))
        return out

    def cut(position, *after):
        return call(cut_kernel, [half], [], [position, tile, *after])[0]

    place = lax.axis_index("depth").astype(jnp.int32).reshape(1)
    parity = (lax.axis_index("probe").astype(jnp.int32) & 1).reshape(1)
    prop, dft = [jnp.asarray(x) for x in tables(extent)]

    before = step(positions, 1)
    after = step(positions, -1)
    (tile,) = pl.pallas_call(
        tile_kernel,
        out_shape=[pltpu.VMEM(potential.shape, f32)],
        in_specs=[ANY],
        out_specs=[VMEM],
        scratch_shapes=[pltpu.SemaphoreType.DMA((8,))],
        name="tile",
    )(potential)
    for_before = cut(before)
    below = step(for_before, -1)
    for_after = cut(after, for_before)
    above = step(for_after, 1)
    own = cut(positions, for_after)
    owns = to_depths(own)
    upper, wave = call(
        first_kernel,
        [(layers, 2, strip, extent), field],
        [positions],
        [own, probe, prop],
    )
    other = call(merge_kernel, [half[1:]] * layers, [], [positions, above, below, wave])
    others = []
    for layer in range(layers):
        others.append(to_depths(other[layer]))
    wave, table, saved = call(
        functools.partial(enter_kernel, layers),
        [field, (slices, *field), (layers, *field)],
        [place],
        [wave, prop, upper, *other],
        aliases=[(0, 0)],
    )
    wave, table = call(
        functools.partial(middle_kernel, depth_count, layers),
        [field, table.shape],
        [place],
        [wave, prop, table, *owns, *others[0]],
        aliases=[(0, 0), (2, 1)],
    )
    rest = [others[layer][k] for k in range(depth_count - 1) for layer in range(1, layers)]
    mine, outer, _, _ = call(
        functools.partial(solve_kernel, depth_count),
        [half, half, table.shape, saved.shape],
        [place],
        [wave, saved, intensity, prop, dft, table, *owns, *rest],
        aliases=[(5, 2), (1, 3)],
    )
    odd = parity[0] == 1
    fast_position = jnp.where(odd, before, after)
    slow_position = jnp.where(odd, after, before)
    fast, slow = swapped(outer, outer)
    (staged,) = call(
        stage_kernel, [potential.shape], [parity], [positions, fast_position, mine, fast]
    )
    arrays = [slow_position, slow, staged]
    arrays = [pltpu.with_memory_space_constraint(x, pltpu.VMEM) for x in arrays]
    return pl.pallas_call(
        place_kernel,
        out_shape=jax.ShapeDtypeStruct(potential.shape, f32),
        in_specs=[SMEM] + [VMEM] * 3,
        out_specs=ANY,
        scratch_shapes=[
            pltpu.VMEM(potential.shape, f32),
            pltpu.SemaphoreType.DMA((columns // extent,)),
        ],
        name="place",
    )(parity, *arrays)


def solution(mesh):
    in_specs = (P("depth", "probe", None), P(), P("probe", None), P("probe", None, None))
    out_specs = P("depth", "probe", None)

    return jax.shard_map(
        local, mesh=mesh, in_specs=in_specs, out_specs=out_specs, check_vma=False
    )
```

```python
import functools

import jax
import jax.numpy as jnp
import numpy as np
from jax import lax
from jax.experimental import pallas as pl
from jax.experimental.pallas import tpu as pltpu
from jax.sharding import PartitionSpec as P

interaction = 0.5
fresnel_phase = 60.0
f32 = jnp.float32
bf16 = jnp.bfloat16

VMEM = pl.BlockSpec(memory_space=pltpu.VMEM)
SMEM = pl.BlockSpec(memory_space=pltpu.SMEM)
ANY = pl.BlockSpec(memory_space=pl.ANY)


def poly_tables():
    v = np.cos(np.linspace(0.0, np.pi / 2, 4001)) * 6.01
    h = interaction * v / 2
    fit = np.polynomial.chebyshev.Chebyshev.fit
    kind = np.polynomial.Polynomial
    sine = fit(v * v, interaction * np.sinc(h / np.pi), 4).convert(kind=kind).coef
    cosine = fit(v * v, np.cos(h), 5).convert(kind=kind).coef
    return [float(x) for x in sine], [float(x) for x in cosine]


def split_table(matrix):
    parts = []
    for real in (matrix.real, matrix.imag, -matrix.imag):
        wide = real.astype(np.float32)
        high = wide.astype(bf16)
        parts.append(high)
        parts.append((real - high.astype(np.float64)).astype(np.float32).astype(bf16))
    return np.stack(parts)


def tables(extent):
    index = np.arange(extent)
    dft = np.exp(-2j * np.pi * ((index[:, None] * index[None, :]) % extent) / extent)
    dft = dft / np.sqrt(extent)
    frequency = ((index + extent // 2) % extent - extent // 2) / extent
    chirp = np.exp(-1j * fresnel_phase * frequency**2)
    propagator = np.conj(dft) @ (chirp[:, None] * dft)
    return split_table(propagator), split_table(dft)


def sin_cos(window):
    sine, cosine = poly_tables()
    z = window * window
    s = sine[-1]
    for k in sine[-2::-1]:
        s = s * z + k
    s = s * window
    c = cosine[-1]
    for k in cosine[-2::-1]:
        c = c * z + k
    return s * c, 1.0 - (0.5 * s) * s


def parts_of(x):
    high = x.astype(bf16)
    return high, (x - high.astype(f32)).astype(bf16)


def dot(a, b):
    return jnp.dot(a, b, preferred_element_type=f32)


def sandwich(m, real, imag):
    m = [m[k] for k in range(6)]
    rows = jnp.concatenate
    rh, rl = parts_of(real)
    ih, il = parts_of(imag)
    left = rows([rh, rl, rh, ih, il, ih], axis=1)
    yr = dot(left, rows([m[0], m[0], m[1], m[4], m[4], m[5]], axis=0))
    yi = dot(left, rows([m[2], m[2], m[3], m[0], m[0], m[1]], axis=0))
    rh, rl = parts_of(yr)
    ih, il = parts_of(yi)
    right = rows([rh, rl, rh, ih, il, ih], axis=0)
    zr = dot(rows([m[0], m[0], m[1], m[4], m[4], m[5]], axis=1), right)
    zi = dot(rows([m[2], m[2], m[3], m[0], m[0], m[1]], axis=1), right)
    return zr, zi


def call(kernel, results, scalars, arrays, aliases=(), scratch=(), limit=4):
    arrays = [pltpu.with_memory_space_constraint(x, pltpu.VMEM) for x in arrays]
    return pl.pallas_call(
        kernel,
        out_shape=[pltpu.VMEM(shape, f32) for shape in results],
        in_specs=[SMEM] * len(scalars) + [VMEM] * len(arrays),
        out_specs=[VMEM] * len(results),
        input_output_aliases={len(scalars) + i: o for i, o in aliases},
        scratch_shapes=list(scratch),
        compiler_params=pltpu.CompilerParams(vmem_limit_bytes=limit * 2**20),
    )(*scalars, *arrays)


def entry(position, k):
    return position[0:1, k : k + 1]


def covered(column, block, shape):
    lane = lax.broadcasted_iota(jnp.int32, shape, 1) + block * shape[1]
    return (lane >= column) & (lane < column + shape[1])


def fold_columns(potential, position, out):
    layers, strip, columns = potential.shape
    extent = 2 * strip
    column = entry(position, 1)
    for layer in range(layers):
        value = potential[layer, :, :extent]
        for block in range(1, columns // extent):
            mask = covered(column, block, value.shape)
            next_value = potential[layer, :, block * extent : (block + 1) * extent]
            value = jnp.where(mask, next_value, value)
        out[layer][...] = value


def tile_kernel(potential, tile, sems):
    copies = []
    for layer in range(potential.shape[0]):
        copies.append(pltpu.make_async_copy(potential.at[layer], tile.at[layer], sems.at[layer]))
        copies[layer].start()
    for copy in copies:
        copy.wait()


def cut_kernel(position, tile, *refs):
    layers = tile.shape[0]
    whole = len(refs[-1].shape) == 3
    outs = [refs[-1].at[layer] for layer in range(layers)] if whole else refs[-layers:]
    fold_columns(tile, position, outs)


def fill(table, slices, rows, piece):
    for layer, at in enumerate(slices):
        s, c = sin_cos(piece(layer))
        table[at, 0, rows] = c
        table[at, 1, rows] = s


def slices_of(depth, k, count, layers):
    first = (depth - k + count) % count * layers
    return [first + layer for layer in range(layers)]


def first_kernel(position, probe, _, own, upper, wave):
    layers, strip, _ = own.shape
    row_shift = position[0, 0] % strip + strip
    column_shift = position[0, 1] % (2 * strip)
    for k in range(2):
        wave[k] = pltpu.roll(pltpu.roll(probe[k], row_shift, 0), column_shift, 1)
    fill(upper, range(layers), slice(0, strip), lambda layer: own[layer])


def merge_kernel(layer, position, above, below, _, out):
    row = lax.broadcasted_iota(jnp.int32, above.shape, 0)
    mask = row >= entry(position, 0) % above.shape[0]
    out[...] = jnp.where(mask, above[...], below[layer])


def transmit(trans, real, imag):
    c, s = trans
    return c * real - s * imag, c * imag + s * real


def enter_kernel(layers, place, wave_in, prop, upper, *refs):
    others = refs[:layers]
    wave_out, table, saved = refs[layers:]
    strip, extent = others[0].shape
    slices = [place[0] * layers + layer for layer in range(layers)]
    for layer in range(layers):
        for part in range(2):
            table[slices[layer], part, :strip] = upper[layer, part]
    fill(table, slices, slice(strip, extent), lambda layer: others[layer][...])

    def forward(layer, wave):
        wave = transmit((table[layer, 0], table[layer, 1]), *wave)
        saved[layer, 0] = wave[0]
        saved[layer, 1] = wave[1]
        return sandwich(prop, *wave)

    @pl.when(place[0] == 0)
    def _():
        wave = lax.fori_loop(0, layers, forward, (wave_in[0], wave_in[1]))
        wave_out[0] = wave[0]
        wave_out[1] = wave[1]


def middle_kernel(count, layers, place, wave_in, prop, table_in, *refs):
    owns = refs[: count - 1]
    others = refs[count - 1 : 2 * count - 2]
    wave_out, table = refs[2 * count - 2 :]
    strip, extent = others[0].shape
    owners = [slices_of(place[0], k, count, layers)[0] for k in range(1, count)]
    fill(table, owners, slice(0, strip), lambda k: owns[k][0])
    fill(table, owners, slice(strip, extent), lambda k: others[k][...])
    s = jnp.where(place[0] == 0, layers, 0)
    wave = transmit((table[s, 0], table[s, 1]), wave_in[0], wave_in[1])
    wave_out[0], wave_out[1] = sandwich(prop, *wave)


def solve_kernel(count, place, wave_in, saved_in, intensity, prop, dft, table_in, *refs):
    mine, outer, table, saved = refs[-4:]
    layers, strip, extent = mine.shape
    slices = layers * count
    last = slices - 1
    depth = place[0]
    first = depth * layers
    for k in range(1, count):
        own = refs[(k - 1) * layers]
        others = refs[(k - 1) * layers + 1 : k * layers]
        owners = slices_of(depth, k, count, layers)[1:]
        fill(table, owners, slice(0, strip), lambda layer: own[layer + 1])
        fill(table, owners, slice(strip, extent), lambda layer: others[layer][...])

    def enter(s, wave):
        wave = transmit((table[s, 0], table[s, 1]), *wave)

        @pl.when((s >= first) & (s < first + layers))
        def _():
            saved[s - first, 0] = wave[0]
            saved[s - first, 1] = wave[1]

        return wave

    wave = (wave_in[0], wave_in[1])
    start = jnp.where(depth == 0, layers + 1, 1)
    wave = lax.fori_loop(start, last, lambda s, w: sandwich(prop, *enter(s, w)), wave)
    far_real, far_imag = sandwich(dft, *enter(last, wave))
    misfit = far_real * far_real + far_imag * far_imag - intensity[0]
    wave = sandwich(dft, misfit * far_real, -(misfit * far_imag))

    def term(s, wave):
        @pl.when(s < first + layers)
        def _():
            value = wave[1] * saved[s - first, 0] + wave[0] * saved[s - first, 1]
            value = -interaction * value
            mine[s - first] = value[:strip]
            outer[s - first] = value[strip:]

    term(last, wave)

    def backward(step, wave):
        s = last - step
        wave = sandwich(prop, *transmit((table[s, 0], table[s, 1]), *wave))
        term(s - 1, wave)
        return wave

    lax.fori_loop(0, last - first, backward, wave)


def covers(position, block, shape, odd):
    strip = shape[0]
    row = lax.broadcasted_iota(jnp.int32, shape, 0)
    rows = (row >= entry(position, 0) % strip).astype(jnp.int32) != odd
    return covered(entry(position, 1), block, shape) & rows


def stage_kernel(parity, position, fast_position, mine, fast, staged):
    layers, strip, columns = staged.shape
    extent = 2 * strip
    shape = (strip, extent)
    for block in range(columns // extent):
        at = slice(block * extent, (block + 1) * extent)
        own = covered(entry(position, 1), block, shape)
        near = covers(fast_position, block, shape, parity[0])
        for layer in range(layers):
            value = jnp.where(own, mine[layer], 0.0) + jnp.where(near, fast[layer], 0.0)
            staged[layer, :, at] = value


def place_kernel(parity, slow_position, slow, staged, out, final, sems):
    layers, strip, columns = out.shape
    extent = 2 * strip
    copies = []
    for block in range(columns // extent):
        at = slice(block * extent, (block + 1) * extent)
        far = covers(slow_position, block, (strip, extent), 1 - parity[0])
        for layer in range(layers):
            value = staged[layer, :, at] + jnp.where(far, slow[layer], 0.0)
            final[layer, :, at] = value
        copy = pltpu.make_async_copy(final.at[:, :, at], out.at[:, :, at], sems.at[block])
        copy.start()
        copies.append(copy)
    for copy in copies:
        copy.wait()


def local(potential, probe, positions, intensity):
    layers, strip, columns = potential.shape
    extent = probe.shape[1]
    count = lax.axis_size("probe")
    depth_count = lax.axis_size("depth")
    assert positions.shape[0] == 1 and extent == 2 * strip and columns % extent == 0
    assert count % 2 == 0 and layers * (depth_count - 1) > 1
    slices = layers * depth_count
    half = (layers, strip, extent)
    field = (2, extent, extent)
    fast_pairs = [(i, i ^ 1) for i in range(count)]
    slow_pairs = [(i, (i + 1 if i % 2 else i - 1) % count) for i in range(count)]

    def swapped(fast, slow):
        slow = lax.ppermute(slow, "probe", slow_pairs)
        return lax.ppermute(fast, "probe", fast_pairs), slow

    def step(x, by):
        return lax.ppermute(x, "probe", [(i, (i + by) % count) for i in range(count)])

    def to_depths(x):
        out = []
        for k in range(1, depth_count):
            pairs = [(i, (i + k) % depth_count) for i in range(depth_count)]
            out.append(lax.ppermute(x, "depth", pairs))
        return out

    def cut(shapes, position, *after):
        return call(cut_kernel, shapes, [], [position, tile, *after])

    place = lax.axis_index("depth").astype(jnp.int32).reshape(1)
    parity = (lax.axis_index("probe").astype(jnp.int32) & 1).reshape(1)
    prop, dft = [jnp.asarray(x) for x in tables(extent)]

    before = step(positions, 1)
    after = step(positions, -1)
    (tile,) = pl.pallas_call(
        tile_kernel,
        out_shape=[pltpu.VMEM(potential.shape, f32)],
        in_specs=[ANY],
        out_specs=[VMEM],
        scratch_shapes=[pltpu.SemaphoreType.DMA((layers,))],
        name="tile",
    )(potential)

    def by_layer(pieces, send):
        out = []
        for layer in range(layers):
            out.append(send(pieces[layer]))
        return out

    (for_before,) = cut([half], before)
    below = step(for_before, -1)
    for_after = cut([half[1:]] * layers, after, for_before)
    above = by_layer(for_after, lambda x: step(x, 1))
    (own,) = cut([half], positions, *for_after)
    owns = to_depths(own)
    upper, wave = call(
        first_kernel,
        [(layers, 2, strip, extent), field],
        [positions],
        [probe, prop, own],
    )
    other = []
    for layer in range(layers):
        arrays = [positions, above[layer], below, wave]
        kernel = functools.partial(merge_kernel, layer)
        other += call(kernel, [half[1:]], [], arrays)
    others = by_layer(other, to_depths)
    wave, table, saved = call(
        functools.partial(enter_kernel, layers),
        [field, (slices, *field), (layers, *field)],
        [place],
        [wave, prop, upper, *other],
        aliases=[(0, 0)],
    )
    wave, table = call(
        functools.partial(middle_kernel, depth_count, layers),
        [field, table.shape],
        [place],
        [wave, prop, table, *owns, *others[0]],
        aliases=[(0, 0), (2, 1)],
    )
    rest = []
    for k in range(depth_count - 1):
        rest += [owns[k], *[others[layer][k] for layer in range(1, layers)]]
    mine, outer, _, _ = call(
        functools.partial(solve_kernel, depth_count),
        [half, half, table.shape, saved.shape],
        [place],
        [wave, saved, intensity, prop, dft, table, *rest],
        aliases=[(5, 2), (1, 3)],
    )
    odd = parity[0] == 1
    fast_position = jnp.where(odd, before, after)
    slow_position = jnp.where(odd, after, before)
    fast, slow = swapped(outer, outer)
    (staged,) = call(
        stage_kernel, [potential.shape], [parity], [positions, fast_position, mine, fast]
    )
    arrays = [slow_position, slow, staged]
    arrays = [pltpu.with_memory_space_constraint(x, pltpu.VMEM) for x in arrays]
    return pl.pallas_call(
        place_kernel,
        out_shape=jax.ShapeDtypeStruct(potential.shape, f32),
        in_specs=[SMEM] + [VMEM] * 3,
        out_specs=ANY,
        scratch_shapes=[
            pltpu.VMEM(potential.shape, f32),
            pltpu.SemaphoreType.DMA((columns // extent,)),
        ],
        name="place",
    )(parity, *arrays)


def solution(mesh):
    in_specs = (P("depth", "probe", None), P(), P("probe", None), P("probe", None, None))
    out_specs = P("depth", "probe", None)

    return jax.shard_map(
        local, mesh=mesh, in_specs=in_specs, out_specs=out_specs, check_vma=False
    )
```

```python
import functools

import jax
import jax.numpy as jnp
import numpy as np
from jax import lax
from jax.experimental import pallas as pl
from jax.experimental.pallas import tpu as pltpu
from jax.sharding import PartitionSpec as P


interaction = 0.5
fresnel_phase = 60.0
f32 = jnp.float32
bf16 = jnp.bfloat16

VMEM = pl.BlockSpec(memory_space=pltpu.VMEM)
SMEM = pl.BlockSpec(memory_space=pltpu.SMEM)
ANY = pl.BlockSpec(memory_space=pl.ANY)


def poly_tables():
    v = np.cos(np.linspace(0.0, np.pi / 2, 4001)) * 6.01
    h = interaction * v / 2
    fit = np.polynomial.chebyshev.Chebyshev.fit
    kind = np.polynomial.Polynomial
    sine = fit(v * v, interaction * np.sinc(h / np.pi), 4).convert(kind=kind).coef
    cosine = fit(v * v, np.cos(h), 5).convert(kind=kind).coef
    return [float(x) for x in sine], [float(x) for x in cosine]


def split_table(matrix):
    parts = []
    for real in (matrix.real, matrix.imag, -matrix.imag):
        wide = real.astype(np.float32)
        high = wide.astype(bf16)
        parts.append(high)
        parts.append((real - high.astype(np.float64)).astype(np.float32).astype(bf16))
    return np.stack(parts)


def tables(extent):
    index = np.arange(extent)
    dft = np.exp(-2j * np.pi * ((index[:, None] * index[None, :]) % extent) / extent)
    dft = dft / np.sqrt(extent)
    frequency = ((index + extent // 2) % extent - extent // 2) / extent
    chirp = np.exp(-1j * fresnel_phase * frequency**2)
    propagator = np.conj(dft) @ (chirp[:, None] * dft)
    return split_table(propagator), split_table(dft)


def sin_cos(window):
    sine, cosine = poly_tables()
    z = window * window
    s = sine[-1]
    for k in sine[-2::-1]:
        s = s * z + k
    s = s * window
    c = cosine[-1]
    for k in cosine[-2::-1]:
        c = c * z + k
    return s * c, 1.0 - (0.5 * s) * s


def parts_of(x):
    high = x.astype(bf16)
    return high, (x - high.astype(f32)).astype(bf16)


def dot(a, b):
    return jnp.dot(a, b, preferred_element_type=f32)


def sandwich(m, real, imag):
    m = [m[k] for k in range(6)]
    rows = jnp.concatenate
    rh, rl = parts_of(real)
    ih, il = parts_of(imag)
    left = rows([rh, rl, rh, ih, il, ih], axis=1)
    yr = dot(left, rows([m[0], m[0], m[1], m[4], m[4], m[5]], axis=0))
    yi = dot(left, rows([m[2], m[2], m[3], m[0], m[0], m[1]], axis=0))
    rh, rl = parts_of(yr)
    ih, il = parts_of(yi)
    right = rows([rh, rl, rh, ih, il, ih], axis=0)
    zr = dot(rows([m[0], m[0], m[1], m[4], m[4], m[5]], axis=1), right)
    zi = dot(rows([m[2], m[2], m[3], m[0], m[0], m[1]], axis=1), right)
    return zr, zi


def call(kernel, results, scalars, arrays, aliases=(), scratch=(), limit=4):
    arrays = [pltpu.with_memory_space_constraint(x, pltpu.VMEM) for x in arrays]
    return pl.pallas_call(
        kernel,
        out_shape=[pltpu.VMEM(shape, f32) for shape in results],
        in_specs=[SMEM] * len(scalars) + [VMEM] * len(arrays),
        out_specs=[VMEM] * len(results),
        input_output_aliases={len(scalars) + i: o for i, o in aliases},
        scratch_shapes=list(scratch),
        compiler_params=pltpu.CompilerParams(vmem_limit_bytes=limit * 2**20),
    )(*scalars, *arrays)


def entry(position, k):
    return position[0:1, k : k + 1]


def covered(column, block, shape):
    lane = lax.broadcasted_iota(jnp.int32, shape, 1) + block * shape[1]
    return (lane >= column) & (lane < column + shape[1])


def fold_columns(potential, position, out):
    layers, strip, columns = potential.shape
    extent = 2 * strip
    column = entry(position, 1)
    for layer in range(layers):
        value = potential[layer, :, :extent]
        for block in range(1, columns // extent):
            mask = covered(column, block, value.shape)
            next_value = potential[layer, :, block * extent : (block + 1) * extent]
            value = jnp.where(mask, next_value, value)
        out[layer][...] = value


def tile_kernel(potential, tile, sems):
    copies = []
    for layer in range(potential.shape[0]):
        copies.append(pltpu.make_async_copy(potential.at[layer], tile.at[layer], sems.at[layer]))
        copies[layer].start()
    for copy in copies:
        copy.wait()


def cut_kernel(position, tile, *refs):
    layers = tile.shape[0]
    whole = len(refs[-1].shape) == 3
    outs = [refs[-1].at[layer] for layer in range(layers)] if whole else refs[-layers:]
    fold_columns(tile, position, outs)


def fill(table, slices, rows, piece):
    for layer, at in enumerate(slices):
        s, c = sin_cos(piece(layer))
        table[at, 0, rows] = c
        table[at, 1, rows] = s


def slices_of(depth, k, count, layers):
    first = (depth - k + count) % count * layers
    return [first + layer for layer in range(layers)]


def first_kernel(position, probe, _, own, upper, wave):
    layers, strip, _ = own.shape
    row_shift = position[0, 0] % strip + strip
    column_shift = position[0, 1] % (2 * strip)
    for k in range(2):
        wave[k] = pltpu.roll(pltpu.roll(probe[k], row_shift, 0), column_shift, 1)
    fill(upper, range(layers), slice(0, strip), lambda layer: own[layer])


def merge_kernel(layer, position, above, below, _, out):
    row = lax.broadcasted_iota(jnp.int32, above.shape, 0)
    mask = row >= entry(position, 0) % above.shape[0]
    out[...] = jnp.where(mask, above[...], below[layer])


def transmit(trans, real, imag):
    c, s = trans
    return c * real - s * imag, c * imag + s * real


def enter_kernel(layers, place, wave_in, prop, upper, *refs):
    others = refs[:layers]
    wave_out, table, saved = refs[layers:]
    strip, extent = others[0].shape
    slices = [place[0] * layers + layer for layer in range(layers)]
    for layer in range(layers):
        for part in range(2):
            table[slices[layer], part, :strip] = upper[layer, part]
    fill(table, slices, slice(strip, extent), lambda layer: others[layer][...])

    def forward(layer, wave):
        wave = transmit((table[layer, 0], table[layer, 1]), *wave)
        saved[layer, 0] = wave[0]
        saved[layer, 1] = wave[1]
        return sandwich(prop, *wave)

    @pl.when(place[0] == 0)
    def _():
        wave = lax.fori_loop(0, layers, forward, (wave_in[0], wave_in[1]))
        wave_out[0] = wave[0]
        wave_out[1] = wave[1]


def middle_kernel(count, layers, place, wave_in, prop, table_in, *refs):
    owns = refs[: count - 1]
    others = refs[count - 1 : 2 * count - 2]
    wave_out, table = refs[2 * count - 2 :]
    strip, extent = others[0].shape
    owners = [slices_of(place[0], k, count, layers)[0] for k in range(1, count)]
    fill(table, owners, slice(0, strip), lambda k: owns[k][0])
    fill(table, owners, slice(strip, extent), lambda k: others[k][...])
    s = jnp.where(place[0] == 0, layers, 0)
    wave = transmit((table[s, 0], table[s, 1]), wave_in[0], wave_in[1])
    wave_out[0], wave_out[1] = sandwich(prop, *wave)


def solve_kernel(count, turn, place, parity, wave_in, saved_in, intensity, prop, dft, table_in, *refs):
    mine, outer, table, saved = refs[-4:]
    if turn == 0:
        before = refs[-5]

        @pl.when(parity[0] != turn)
        def _():
            outer[...] = before[...]

    @pl.when(parity[0] == turn)
    def _():
        layers, strip, extent = mine.shape
        slices = layers * count
        last = slices - 1
        depth = place[0]
        first = depth * layers
        for k in range(1, count):
            own = refs[(k - 1) * layers]
            others = refs[(k - 1) * layers + 1 : k * layers]
            owners = slices_of(depth, k, count, layers)[1:]
            fill(table, owners, slice(0, strip), lambda layer: own[layer + 1])
            fill(table, owners, slice(strip, extent), lambda layer: others[layer][...])

        def enter(s, wave):
            wave = transmit((table[s, 0], table[s, 1]), *wave)

            @pl.when((s >= first) & (s < first + layers))
            def _():
                saved[s - first, 0] = wave[0]
                saved[s - first, 1] = wave[1]

            return wave

        wave = (wave_in[0], wave_in[1])
        start = jnp.where(depth == 0, layers + 1, 1)
        wave = lax.fori_loop(start, last, lambda s, w: sandwich(prop, *enter(s, w)), wave)
        far_real, far_imag = sandwich(dft, *enter(last, wave))
        misfit = far_real * far_real + far_imag * far_imag - intensity[0]
        wave = sandwich(dft, misfit * far_real, -(misfit * far_imag))

        def term(s, wave):
            @pl.when(s < first + layers)
            def _():
                value = wave[1] * saved[s - first, 0] + wave[0] * saved[s - first, 1]
                value = -interaction * value
                mine[s - first] = value[:strip]
                outer[s - first] = value[strip:]

        term(last, wave)

        def backward(step, wave):
            s = last - step
            wave = sandwich(prop, *transmit((table[s, 0], table[s, 1]), *wave))
            term(s - 1, wave)
            return wave

        lax.fori_loop(0, last - first, backward, wave)


def covers(position, block, shape, odd):
    strip = shape[0]
    row = lax.broadcasted_iota(jnp.int32, shape, 0)
    rows = (row >= entry(position, 0) % strip).astype(jnp.int32) != odd
    return covered(entry(position, 1), block, shape) & rows


def stage_kernel(parity, position, fast_position, mine, fast, staged):
    layers, strip, columns = staged.shape
    extent = 2 * strip
    shape = (strip, extent)
    for block in range(columns // extent):
        at = slice(block * extent, (block + 1) * extent)
        own = covered(entry(position, 1), block, shape)
        near = covers(fast_position, block, shape, parity[0])
        for layer in range(layers):
            value = jnp.where(own, mine[layer], 0.0) + jnp.where(near, fast[layer], 0.0)
            staged[layer, :, at] = value


def place_kernel(parity, slow_position, from_odd, from_even, staged, out, final, sems):
    layers, strip, columns = out.shape
    extent = 2 * strip
    slow = [from_odd[layer] + from_even[layer] for layer in range(layers)]
    copies = []
    for block in range(columns // extent):
        at = slice(block * extent, (block + 1) * extent)
        far = covers(slow_position, block, (strip, extent), 1 - parity[0])
        for layer in range(layers):
            value = staged[layer, :, at] + jnp.where(far, slow[layer], 0.0)
            final[layer, :, at] = value
        copy = pltpu.make_async_copy(final.at[:, :, at], out.at[:, :, at], sems.at[block])
        copy.start()
        copies.append(copy)
    for copy in copies:
        copy.wait()


def local(potential, probe, positions, intensity):
    layers, strip, columns = potential.shape
    extent = probe.shape[1]
    count = lax.axis_size("probe")
    depth_count = lax.axis_size("depth")
    assert positions.shape[0] == 1 and extent == 2 * strip and columns % extent == 0
    assert count % 2 == 0 and layers * (depth_count - 1) > 1
    slices = layers * depth_count
    half = (layers, strip, extent)
    field = (2, extent, extent)
    fast_pairs = [(i, i ^ 1) for i in range(count)]
    slow_pairs = [(i, (i + 1 if i % 2 else i - 1) % count) for i in range(count)]

    def step(x, by):
        return lax.ppermute(x, "probe", [(i, (i + by) % count) for i in range(count)])

    def to_depths(x):
        out = []
        for k in range(1, depth_count):
            pairs = [(i, (i + k) % depth_count) for i in range(depth_count)]
            out.append(lax.ppermute(x, "depth", pairs))
        return out

    def cut(shapes, position, *after):
        return call(cut_kernel, shapes, [], [position, tile, *after])

    place = lax.axis_index("depth").astype(jnp.int32).reshape(1)
    parity = (lax.axis_index("probe").astype(jnp.int32) & 1).reshape(1)
    prop, dft = [jnp.asarray(x) for x in tables(extent)]

    before = step(positions, 1)
    after = step(positions, -1)
    (tile,) = pl.pallas_call(
        tile_kernel,
        out_shape=[pltpu.VMEM(potential.shape, f32)],
        in_specs=[ANY],
        out_specs=[VMEM],
        scratch_shapes=[pltpu.SemaphoreType.DMA((layers,))],
        name="tile",
    )(potential)

    def by_layer(pieces, send):
        out = []
        for layer in range(layers):
            out.append(send(pieces[layer]))
        return out

    (for_before,) = cut([half], before)
    below = step(for_before, -1)
    (own,) = cut([half], positions, for_before)
    owns = to_depths(own)
    for_after = cut([half[1:]] * layers, after, own)
    above = by_layer(for_after, lambda x: step(x, 1))
    upper, wave = call(
        first_kernel,
        [(layers, 2, strip, extent), field],
        [positions],
        [probe, prop, own],
    )
    other = []
    for layer in range(layers):
        arrays = [positions, above[layer], below, wave]
        kernel = functools.partial(merge_kernel, layer)
        other += call(kernel, [half[1:]], [], arrays)
    others = by_layer(other, to_depths)
    wave, table, saved = call(
        functools.partial(enter_kernel, layers),
        [field, (slices, *field), (layers, *field)],
        [place],
        [wave, prop, upper, *other],
        aliases=[(0, 0)],
    )
    wave, table = call(
        functools.partial(middle_kernel, depth_count, layers),
        [field, table.shape],
        [place],
        [wave, prop, table, *owns, *others[0]],
        aliases=[(0, 0), (2, 1)],
    )
    rest = []
    for k in range(depth_count - 1):
        rest += [owns[k], *[others[layer][k] for layer in range(1, layers)]]

    def solve(turn, table, saved, *earlier):
        rest_refs = 6 + len(rest)
        return call(
            functools.partial(solve_kernel, depth_count, turn),
            [half, half, table.shape, saved.shape],
            [place, parity],
            [wave, saved, intensity, prop, dft, table, *rest, *earlier],
            aliases=[(5, 2), (1, 3)] + ([(rest_refs, 0)] if earlier else []),
            limit=4 * (depth_count - 1),
        )

    odd_groups = [(i, j) for i, j in slow_pairs if i % 2 == 1]
    even_groups = [(i, j) for i, j in slow_pairs if i % 2 == 0]
    mine, outer, table, saved = solve(1, table, saved)
    from_odd = lax.ppermute(outer, "probe", odd_groups)
    mine, outer, _, _ = solve(0, table, saved, mine, outer)
    from_even = lax.ppermute(outer, "probe", even_groups)
    fast = lax.ppermute(outer, "probe", fast_pairs)
    odd = parity[0] == 1
    fast_position = jnp.where(odd, before, after)
    slow_position = jnp.where(odd, after, before)
    (staged,) = call(
        stage_kernel, [potential.shape], [parity], [positions, fast_position, mine, fast]
    )
    arrays = [slow_position, from_odd, from_even, staged]
    arrays = [pltpu.with_memory_space_constraint(x, pltpu.VMEM) for x in arrays]
    return pl.pallas_call(
        place_kernel,
        out_shape=jax.ShapeDtypeStruct(potential.shape, f32),
        in_specs=[SMEM] + [VMEM] * 4,
        out_specs=ANY,
        scratch_shapes=[
            pltpu.VMEM(potential.shape, f32),
            pltpu.SemaphoreType.DMA((columns // extent,)),
        ],
        name="place",
    )(parity, *arrays)


def solution(mesh):
    in_specs = (P("depth", "probe", None), P(), P("probe", None), P("probe", None, None))
    out_specs = P("depth", "probe", None)

    return jax.shard_map(
        local, mesh=mesh, in_specs=in_specs, out_specs=out_specs, check_vma=False
    )
```

```python
import functools

import jax
import jax.numpy as jnp
import numpy as np
from jax import lax
from jax.experimental import pallas as pl
from jax.experimental.pallas import tpu as pltpu
from jax.sharding import PartitionSpec as P


interaction = 0.5
fresnel_phase = 60.0
f32 = jnp.float32
bf16 = jnp.bfloat16

VMEM = pl.BlockSpec(memory_space=pltpu.VMEM)
SMEM = pl.BlockSpec(memory_space=pltpu.SMEM)
ANY = pl.BlockSpec(memory_space=pl.ANY)


def poly_tables():
    v = np.cos(np.linspace(0.0, np.pi / 2, 4001)) * 6.01
    h = interaction * v / 2
    fit = np.polynomial.chebyshev.Chebyshev.fit
    kind = np.polynomial.Polynomial
    sine = fit(v * v, interaction * np.sinc(h / np.pi), 4).convert(kind=kind).coef
    cosine = fit(v * v, np.cos(h), 5).convert(kind=kind).coef
    return [float(x) for x in sine], [float(x) for x in cosine]


def split_table(matrix):
    parts = []
    for real in (matrix.real, matrix.imag, -matrix.imag):
        wide = real.astype(np.float32)
        high = wide.astype(bf16)
        parts.append(high)
        parts.append((real - high.astype(np.float64)).astype(np.float32).astype(bf16))
    return np.stack(parts)


def tables(extent):
    index = np.arange(extent)
    dft = np.exp(-2j * np.pi * ((index[:, None] * index[None, :]) % extent) / extent)
    dft = dft / np.sqrt(extent)
    frequency = ((index + extent // 2) % extent - extent // 2) / extent
    chirp = np.exp(-1j * fresnel_phase * frequency**2)
    propagator = np.conj(dft) @ (chirp[:, None] * dft)
    return split_table(propagator), split_table(dft)


def sin_cos(window):
    sine, cosine = poly_tables()
    z = window * window
    s = sine[-1]
    for k in sine[-2::-1]:
        s = s * z + k
    s = s * window
    c = cosine[-1]
    for k in cosine[-2::-1]:
        c = c * z + k
    return s * c, 1.0 - (0.5 * s) * s


def parts_of(x):
    high = x.astype(bf16)
    return high, (x - high.astype(f32)).astype(bf16)


def dot(a, b):
    return jnp.dot(a, b, preferred_element_type=f32)


def sandwich(m, real, imag):
    m = [m[k] for k in range(6)]
    rows = jnp.concatenate
    rh, rl = parts_of(real)
    ih, il = parts_of(imag)
    left = rows([rh, rl, rh, ih, il, ih], axis=1)
    yr = dot(left, rows([m[0], m[0], m[1], m[4], m[4], m[5]], axis=0))
    yi = dot(left, rows([m[2], m[2], m[3], m[0], m[0], m[1]], axis=0))
    rh, rl = parts_of(yr)
    ih, il = parts_of(yi)
    right = rows([rh, rl, rh, ih, il, ih], axis=0)
    zr = dot(rows([m[0], m[0], m[1], m[4], m[4], m[5]], axis=1), right)
    zi = dot(rows([m[2], m[2], m[3], m[0], m[0], m[1]], axis=1), right)
    return zr, zi


def call(kernel, results, scalars, arrays, aliases=(), scratch=(), limit=4):
    arrays = [pltpu.with_memory_space_constraint(x, pltpu.VMEM) for x in arrays]
    return pl.pallas_call(
        kernel,
        out_shape=[pltpu.VMEM(shape, f32) for shape in results],
        in_specs=[SMEM] * len(scalars) + [VMEM] * len(arrays),
        out_specs=[VMEM] * len(results),
        input_output_aliases={len(scalars) + i: o for i, o in aliases},
        scratch_shapes=list(scratch),
        compiler_params=pltpu.CompilerParams(vmem_limit_bytes=limit * 2**20),
    )(*scalars, *arrays)


def entry(position, k):
    return position[0:1, k : k + 1]


def covered(column, block, shape):
    lane = lax.broadcasted_iota(jnp.int32, shape, 1) + block * shape[1]
    return (lane >= column) & (lane < column + shape[1])


def fold_columns(potential, position, out):
    layers, strip, columns = potential.shape
    extent = 2 * strip
    column = entry(position, 1)
    for layer in range(layers):
        value = potential[layer, :, :extent]
        for block in range(1, columns // extent):
            mask = covered(column, block, value.shape)
            next_value = potential[layer, :, block * extent : (block + 1) * extent]
            value = jnp.where(mask, next_value, value)
        out[layer][...] = value


def tile_kernel(potential, tile, sems):
    copies = []
    for layer in range(potential.shape[0]):
        copies.append(pltpu.make_async_copy(potential.at[layer], tile.at[layer], sems.at[layer]))
        copies[layer].start()
    for copy in copies:
        copy.wait()


def cut_kernel(position, tile, *refs):
    layers = tile.shape[0]
    whole = len(refs[-1].shape) == 3
    outs = [refs[-1].at[layer] for layer in range(layers)] if whole else refs[-layers:]
    fold_columns(tile, position, outs)


def fill(table, slices, rows, piece):
    for layer, at in enumerate(slices):
        s, c = sin_cos(piece(layer))
        table[at, 0, rows] = c
        table[at, 1, rows] = s


def slices_of(depth, k, count, layers):
    first = (depth - k + count) % count * layers
    return [first + layer for layer in range(layers)]


def first_kernel(position, probe, _, own, upper, wave):
    layers, strip, _ = own.shape
    row_shift = position[0, 0] % strip + strip
    column_shift = position[0, 1] % (2 * strip)
    for k in range(2):
        wave[k] = pltpu.roll(pltpu.roll(probe[k], row_shift, 0), column_shift, 1)
    fill(upper, range(layers), slice(0, strip), lambda layer: own[layer])


def merge_kernel(layer, position, above, below, _, out):
    row = lax.broadcasted_iota(jnp.int32, above.shape, 0)
    mask = row >= entry(position, 0) % above.shape[0]
    out[...] = jnp.where(mask, above[...], below[layer])


def transmit(trans, real, imag):
    c, s = trans
    return c * real - s * imag, c * imag + s * real


def enter_kernel(layers, place, wave_in, prop, upper, *refs):
    others = refs[:layers]
    wave_out, table, saved = refs[layers:]
    strip, extent = others[0].shape
    slices = [place[0] * layers + layer for layer in range(layers)]
    for layer in range(layers):
        for part in range(2):
            table[slices[layer], part, :strip] = upper[layer, part]
    fill(table, slices, slice(strip, extent), lambda layer: others[layer][...])

    def forward(layer, wave):
        wave = transmit((table[layer, 0], table[layer, 1]), *wave)
        saved[layer, 0] = wave[0]
        saved[layer, 1] = wave[1]
        return sandwich(prop, *wave)

    @pl.when(place[0] == 0)
    def _():
        wave = lax.fori_loop(0, layers, forward, (wave_in[0], wave_in[1]))
        wave_out[0] = wave[0]
        wave_out[1] = wave[1]


def middle_kernel(count, layers, place, wave_in, prop, table_in, *refs):
    owns = refs[: count - 1]
    others = refs[count - 1 : 2 * count - 2]
    wave_out, table = refs[2 * count - 2 :]
    strip, extent = others[0].shape
    owners = [slices_of(place[0], k, count, layers)[0] for k in range(1, count)]
    fill(table, owners, slice(0, strip), lambda k: owns[k][0])
    fill(table, owners, slice(strip, extent), lambda k: others[k][...])
    s = jnp.where(place[0] == 0, layers, 0)
    wave = transmit((table[s, 0], table[s, 1]), wave_in[0], wave_in[1])
    wave_out[0], wave_out[1] = sandwich(prop, *wave)


def solve_kernel(count, turn, place, parity, wave_in, saved_in, intensity, prop, dft, table_in, *refs):
    mine, outer, table, saved = refs[-4:]
    if turn == 0:
        before = refs[-5]

        @pl.when(parity[0] != turn)
        def _():
            outer[...] = before[...]

    @pl.when(parity[0] == turn)
    def _():
        layers, strip, extent = mine.shape
        slices = layers * count
        last = slices - 1
        depth = place[0]
        first = depth * layers
        for k in range(1, count):
            own = refs[(k - 1) * layers]
            others = refs[(k - 1) * layers + 1 : k * layers]
            owners = slices_of(depth, k, count, layers)[1:]
            fill(table, owners, slice(0, strip), lambda layer: own[layer + 1])
            fill(table, owners, slice(strip, extent), lambda layer: others[layer][...])

        def enter(s, wave):
            wave = transmit((table[s, 0], table[s, 1]), *wave)

            @pl.when((s >= first) & (s < first + layers))
            def _():
                saved[s - first, 0] = wave[0]
                saved[s - first, 1] = wave[1]

            return wave

        wave = (wave_in[0], wave_in[1])
        start = jnp.where(depth == 0, layers + 1, 1)
        wave = lax.fori_loop(start, last, lambda s, w: sandwich(prop, *enter(s, w)), wave)
        far_real, far_imag = sandwich(dft, *enter(last, wave))
        misfit = far_real * far_real + far_imag * far_imag - intensity[0]
        wave = sandwich(dft, misfit * far_real, -(misfit * far_imag))

        def term(s, wave):
            @pl.when(s < first + layers)
            def _():
                value = wave[1] * saved[s - first, 0] + wave[0] * saved[s - first, 1]
                value = -interaction * value
                mine[s - first] = value[:strip]
                outer[s - first] = value[strip:]

        term(last, wave)

        def backward(step, wave):
            s = last - step
            wave = sandwich(prop, *transmit((table[s, 0], table[s, 1]), *wave))
            term(s - 1, wave)
            return wave

        lax.fori_loop(0, last - first, backward, wave)


def covers(position, block, shape, odd):
    strip = shape[0]
    row = lax.broadcasted_iota(jnp.int32, shape, 0)
    rows = (row >= entry(position, 0) % strip).astype(jnp.int32) != odd
    return covered(entry(position, 1), block, shape) & rows


def stage_kernel(parity, position, fast_position, mine, fast, staged):
    layers, strip, columns = staged.shape
    extent = 2 * strip
    shape = (strip, extent)
    for block in range(columns // extent):
        at = slice(block * extent, (block + 1) * extent)
        own = covered(entry(position, 1), block, shape)
        near = covers(fast_position, block, shape, parity[0])
        for layer in range(layers):
            value = jnp.where(own, mine[layer], 0.0) + jnp.where(near, fast[layer], 0.0)
            staged[layer, :, at] = value


def place_kernel(parity, slow_position, from_odd, from_even, staged, out, final, sems):
    layers, strip, columns = out.shape
    extent = 2 * strip
    odd = jnp.broadcast_to(parity[0], (strip, extent)) == 1
    slow = [jnp.where(odd, from_even[layer], from_odd[layer]) for layer in range(layers)]
    copies = []
    for block in range(columns // extent):
        at = slice(block * extent, (block + 1) * extent)
        far = covers(slow_position, block, (strip, extent), 1 - parity[0])
        for layer in range(layers):
            value = staged[layer, :, at] + jnp.where(far, slow[layer], 0.0)
            final[layer, :, at] = value
        copy = pltpu.make_async_copy(final.at[:, :, at], out.at[:, :, at], sems.at[block])
        copy.start()
        copies.append(copy)
    for copy in copies:
        copy.wait()


def local(potential, probe, positions, intensity):
    layers, strip, columns = potential.shape
    extent = probe.shape[1]
    count = lax.axis_size("probe")
    depth_count = lax.axis_size("depth")
    assert positions.shape[0] == 1 and extent == 2 * strip and columns % extent == 0
    assert count % 2 == 0 and layers * (depth_count - 1) > 1
    slices = layers * depth_count
    half = (layers, strip, extent)
    field = (2, extent, extent)
    fast_pairs = [(i, i ^ 1) for i in range(count)]
    slow_pairs = [(i, (i + 1 if i % 2 else i - 1) % count) for i in range(count)]

    def step(x, by):
        return lax.ppermute(x, "probe", [(i, (i + by) % count) for i in range(count)])

    def to_depths(x):
        out = []
        for k in range(1, depth_count):
            pairs = [(i, (i + k) % depth_count) for i in range(depth_count)]
            out.append(lax.ppermute(x, "depth", pairs))
        return out

    def cut(shapes, position, *after):
        return call(cut_kernel, shapes, [], [position, tile, *after])

    place = lax.axis_index("depth").astype(jnp.int32).reshape(1)
    parity = (lax.axis_index("probe").astype(jnp.int32) & 1).reshape(1)
    prop, dft = [jnp.asarray(x) for x in tables(extent)]

    before = step(positions, 1)
    after = step(positions, -1)
    (tile,) = pl.pallas_call(
        tile_kernel,
        out_shape=[pltpu.VMEM(potential.shape, f32)],
        in_specs=[ANY],
        out_specs=[VMEM],
        scratch_shapes=[pltpu.SemaphoreType.DMA((layers,))],
        name="tile",
    )(potential)

    def by_layer(pieces, send):
        out = []
        for layer in range(layers):
            out.append(send(pieces[layer]))
        return out

    (for_before,) = cut([half], before)
    below = step(for_before, -1)
    (own,) = cut([half], positions, for_before)
    owns = to_depths(own)
    for_after = cut([half[1:]] * layers, after, own)
    above = by_layer(for_after, lambda x: step(x, 1))
    upper, wave = call(
        first_kernel,
        [(layers, 2, strip, extent), field],
        [positions],
        [probe, prop, own],
    )
    other = []
    for layer in range(layers):
        arrays = [positions, above[layer], below, wave]
        kernel = functools.partial(merge_kernel, layer)
        other += call(kernel, [half[1:]], [], arrays)
    others = by_layer(other, to_depths)
    wave, table, saved = call(
        functools.partial(enter_kernel, layers),
        [field, (slices, *field), (layers, *field)],
        [place],
        [wave, prop, upper, *other],
        aliases=[(0, 0)],
    )
    wave, table = call(
        functools.partial(middle_kernel, depth_count, layers),
        [field, table.shape],
        [place],
        [wave, prop, table, *owns, *others[0]],
        aliases=[(0, 0), (2, 1)],
    )
    rest = []
    for k in range(depth_count - 1):
        rest += [owns[k], *[others[layer][k] for layer in range(1, layers)]]

    def solve(turn, table, saved, *earlier):
        rest_refs = 6 + len(rest)
        return call(
            functools.partial(solve_kernel, depth_count, turn),
            [half, half, table.shape, saved.shape],
            [place, parity],
            [wave, saved, intensity, prop, dft, table, *rest, *earlier],
            aliases=[(5, 2), (1, 3)] + ([(rest_refs, 0)] if earlier else []),
            limit=4 * (depth_count - 1),
        )

    odd_groups = [(i, j) for i, j in slow_pairs if i % 2 == 1]
    even_groups = [fast_pairs[i] if i % 2 else slow_pairs[i] for i in range(count)]
    mine, outer, table, saved = solve(1, table, saved)
    from_odd = lax.ppermute(outer, "probe", odd_groups)
    mine, outer, _, _ = solve(0, table, saved, mine, outer)
    from_even = lax.ppermute(outer, "probe", even_groups)
    fast = lax.ppermute(outer, "probe", fast_pairs)
    odd = parity[0] == 1
    fast_position = jnp.where(odd, before, after)
    slow_position = jnp.where(odd, after, before)
    (staged,) = call(
        stage_kernel, [potential.shape], [parity], [positions, fast_position, mine, fast]
    )
    arrays = [slow_position, from_odd, from_even, staged]
    arrays = [pltpu.with_memory_space_constraint(x, pltpu.VMEM) for x in arrays]
    return pl.pallas_call(
        place_kernel,
        out_shape=jax.ShapeDtypeStruct(potential.shape, f32),
        in_specs=[SMEM] + [VMEM] * 4,
        out_specs=ANY,
        scratch_shapes=[
            pltpu.VMEM(potential.shape, f32),
            pltpu.SemaphoreType.DMA((columns // extent,)),
        ],
        name="place",
    )(parity, *arrays)


def solution(mesh):
    in_specs = (P("depth", "probe", None), P(), P("probe", None), P("probe", None, None))
    out_specs = P("depth", "probe", None)

    return jax.shard_map(
        local, mesh=mesh, in_specs=in_specs, out_specs=out_specs, check_vma=False
    )
```

```python
import functools

import jax
import jax.numpy as jnp
import numpy as np
from jax import lax
from jax.experimental import pallas as pl
from jax.experimental.pallas import tpu as pltpu
from jax.sharding import PartitionSpec as P


interaction = 0.5
fresnel_phase = 60.0
f32 = jnp.float32
bf16 = jnp.bfloat16

VMEM = pl.BlockSpec(memory_space=pltpu.VMEM)
SMEM = pl.BlockSpec(memory_space=pltpu.SMEM)
ANY = pl.BlockSpec(memory_space=pl.ANY)


def poly_tables():
    v = np.cos(np.linspace(0.0, np.pi / 2, 4001)) * 6.01
    h = interaction * v / 2
    fit = np.polynomial.chebyshev.Chebyshev.fit
    kind = np.polynomial.Polynomial
    sine = fit(v * v, interaction * np.sinc(h / np.pi), 4).convert(kind=kind).coef
    cosine = fit(v * v, np.cos(h), 5).convert(kind=kind).coef
    return [float(x) for x in sine], [float(x) for x in cosine]


def split_table(matrix):
    parts = []
    for real in (matrix.real, matrix.imag, -matrix.imag):
        wide = real.astype(np.float32)
        high = wide.astype(bf16)
        parts.append(high)
        parts.append((real - high.astype(np.float64)).astype(np.float32).astype(bf16))
    return np.stack(parts)


def tables(extent):
    index = np.arange(extent)
    dft = np.exp(-2j * np.pi * ((index[:, None] * index[None, :]) % extent) / extent)
    dft = dft / np.sqrt(extent)
    frequency = ((index + extent // 2) % extent - extent // 2) / extent
    chirp = np.exp(-1j * fresnel_phase * frequency**2)
    propagator = np.conj(dft) @ (chirp[:, None] * dft)
    return split_table(propagator), split_table(dft)


def sin_cos(window):
    sine, cosine = poly_tables()
    z = window * window
    s = sine[-1]
    for k in sine[-2::-1]:
        s = s * z + k
    s = s * window
    c = cosine[-1]
    for k in cosine[-2::-1]:
        c = c * z + k
    return s * c, 1.0 - (0.5 * s) * s


def parts_of(x):
    high = x.astype(bf16)
    return high, (x - high.astype(f32)).astype(bf16)


def dot(a, b):
    return jnp.dot(a, b, preferred_element_type=f32)


def sandwich(m, real, imag):
    m = [m[k] for k in range(6)]
    rows = jnp.concatenate
    rh, rl = parts_of(real)
    ih, il = parts_of(imag)
    left = rows([rh, rl, rh, ih, il, ih], axis=1)
    yr = dot(left, rows([m[0], m[0], m[1], m[4], m[4], m[5]], axis=0))
    yi = dot(left, rows([m[2], m[2], m[3], m[0], m[0], m[1]], axis=0))
    rh, rl = parts_of(yr)
    ih, il = parts_of(yi)
    right = rows([rh, rl, rh, ih, il, ih], axis=0)
    zr = dot(rows([m[0], m[0], m[1], m[4], m[4], m[5]], axis=1), right)
    zi = dot(rows([m[2], m[2], m[3], m[0], m[0], m[1]], axis=1), right)
    return zr, zi


def call(kernel, results, scalars, arrays, aliases=(), scratch=(), limit=4):
    arrays = [pltpu.with_memory_space_constraint(x, pltpu.VMEM) for x in arrays]
    return pl.pallas_call(
        kernel,
        out_shape=[pltpu.VMEM(shape, f32) for shape in results],
        in_specs=[SMEM] * len(scalars) + [VMEM] * len(arrays),
        out_specs=[VMEM] * len(results),
        input_output_aliases={len(scalars) + i: o for i, o in aliases},
        scratch_shapes=list(scratch),
        compiler_params=pltpu.CompilerParams(vmem_limit_bytes=limit * 2**20),
    )(*scalars, *arrays)


def entry(position, k):
    return position[0:1, k : k + 1]


def covered(column, block, shape):
    lane = lax.broadcasted_iota(jnp.int32, shape, 1) + block * shape[1]
    return (lane >= column) & (lane < column + shape[1])


def fold_columns(potential, position, out):
    layers, strip, columns = potential.shape
    extent = 2 * strip
    column = entry(position, 1)
    for layer in range(layers):
        value = potential[layer, :, :extent]
        for block in range(1, columns // extent):
            mask = covered(column, block, value.shape)
            next_value = potential[layer, :, block * extent : (block + 1) * extent]
            value = jnp.where(mask, next_value, value)
        out[layer][...] = value


def tile_kernel(potential, tile, sems):
    copies = []
    for layer in range(potential.shape[0]):
        copies.append(pltpu.make_async_copy(potential.at[layer], tile.at[layer], sems.at[layer]))
        copies[layer].start()
    for copy in copies:
        copy.wait()


def cut_kernel(position, tile, *refs):
    layers = tile.shape[0]
    whole = len(refs[-1].shape) == 3
    outs = [refs[-1].at[layer] for layer in range(layers)] if whole else refs[-layers:]
    fold_columns(tile, position, outs)


def fill(table, slices, rows, piece):
    for layer, at in enumerate(slices):
        s, c = sin_cos(piece(layer))
        table[at, 0, rows] = c
        table[at, 1, rows] = s


def slices_of(depth, k, count, layers):
    first = (depth - k + count) % count * layers
    return [first + layer for layer in range(layers)]


def first_kernel(position, probe, _, own, upper, wave):
    layers, strip, _ = own.shape
    row_shift = position[0, 0] % strip + strip
    column_shift = position[0, 1] % (2 * strip)
    for k in range(2):
        wave[k] = pltpu.roll(pltpu.roll(probe[k], row_shift, 0), column_shift, 1)
    fill(upper, range(layers), slice(0, strip), lambda layer: own[layer])


def merge_kernel(layer, position, above, below, _, out):
    row = lax.broadcasted_iota(jnp.int32, above.shape, 0)
    mask = row >= entry(position, 0) % above.shape[0]
    out[...] = jnp.where(mask, above[...], below[layer])


def transmit(trans, real, imag):
    c, s = trans
    return c * real - s * imag, c * imag + s * real


def enter_kernel(layers, place, wave_in, prop, upper, *refs):
    others = refs[:layers]
    wave_out, table, saved = refs[layers:]
    strip, extent = others[0].shape
    slices = [place[0] * layers + layer for layer in range(layers)]
    for layer in range(layers):
        for part in range(2):
            table[slices[layer], part, :strip] = upper[layer, part]
    fill(table, slices, slice(strip, extent), lambda layer: others[layer][...])

    def forward(layer, wave):
        wave = transmit((table[layer, 0], table[layer, 1]), *wave)
        saved[layer, 0] = wave[0]
        saved[layer, 1] = wave[1]
        return sandwich(prop, *wave)

    @pl.when(place[0] == 0)
    def _():
        wave = lax.fori_loop(0, layers, forward, (wave_in[0], wave_in[1]))
        wave_out[0] = wave[0]
        wave_out[1] = wave[1]


def middle_kernel(count, layers, place, wave_in, prop, table_in, *refs):
    owns = refs[: count - 1]
    others = refs[count - 1 : 2 * count - 2]
    wave_out, table = refs[2 * count - 2 :]
    strip, extent = others[0].shape
    owners = [slices_of(place[0], k, count, layers)[0] for k in range(1, count)]
    fill(table, owners, slice(0, strip), lambda k: owns[k][0])
    fill(table, owners, slice(strip, extent), lambda k: others[k][...])
    s = jnp.where(place[0] == 0, layers, 0)
    wave = transmit((table[s, 0], table[s, 1]), wave_in[0], wave_in[1])
    wave_out[0], wave_out[1] = sandwich(prop, *wave)


def solve_kernel(count, turn, place, parity, wave_in, saved_in, intensity, prop, dft, table_in, *refs):
    mine, outer, table, saved = refs[-4:]
    if turn == 0:
        before = refs[-5]

        @pl.when(parity[0] != turn)
        def _():
            outer[...] = before[...]

    @pl.when(parity[0] == turn)
    def _():
        layers, strip, extent = mine.shape
        slices = layers * count
        last = slices - 1
        depth = place[0]
        first = depth * layers
        for k in range(1, count):
            own = refs[(k - 1) * layers]
            others = refs[(k - 1) * layers + 1 : k * layers]
            owners = slices_of(depth, k, count, layers)[1:]
            fill(table, owners, slice(0, strip), lambda layer: own[layer + 1])
            fill(table, owners, slice(strip, extent), lambda layer: others[layer][...])

        def enter(s, wave):
            wave = transmit((table[s, 0], table[s, 1]), *wave)

            @pl.when((s >= first) & (s < first + layers))
            def _():
                saved[s - first, 0] = wave[0]
                saved[s - first, 1] = wave[1]

            return wave

        wave = (wave_in[0], wave_in[1])
        start = jnp.where(depth == 0, layers + 1, 1)
        wave = lax.fori_loop(start, last, lambda s, w: sandwich(prop, *enter(s, w)), wave)
        far_real, far_imag = sandwich(dft, *enter(last, wave))
        misfit = far_real * far_real + far_imag * far_imag - intensity[0]
        wave = sandwich(dft, misfit * far_real, -(misfit * far_imag))

        def term(s, wave):
            @pl.when(s < first + layers)
            def _():
                value = wave[1] * saved[s - first, 0] + wave[0] * saved[s - first, 1]
                value = -interaction * value
                mine[s - first] = value[:strip]
                outer[s - first] = value[strip:]

        term(last, wave)

        def backward(step, wave):
            s = last - step
            wave = sandwich(prop, *transmit((table[s, 0], table[s, 1]), *wave))
            term(s - 1, wave)
            return wave

        lax.fori_loop(0, last - first, backward, wave)


def covers(position, block, shape, odd):
    strip = shape[0]
    row = lax.broadcasted_iota(jnp.int32, shape, 0)
    rows = (row >= entry(position, 0) % strip).astype(jnp.int32) != odd
    return covered(entry(position, 1), block, shape) & rows


def stage_kernel(parity, position, fast_position, mine, fast, staged):
    layers, strip, columns = staged.shape
    extent = 2 * strip
    shape = (strip, extent)
    for block in range(columns // extent):
        at = slice(block * extent, (block + 1) * extent)
        own = covered(entry(position, 1), block, shape)
        near = covers(fast_position, block, shape, parity[0])
        for layer in range(layers):
            value = jnp.where(own, mine[layer], 0.0) + jnp.where(near, fast[layer], 0.0)
            staged[layer, :, at] = value


def place_kernel(parity, slow_position, from_odd, from_even, staged, out, final, sems):
    layers, strip, columns = out.shape
    extent = 2 * strip
    odd = jnp.broadcast_to(parity[0], (strip, extent)) == 1
    row = lax.broadcasted_iota(jnp.int32, (strip, extent), 0)
    rows = (row >= entry(slow_position, 0) % strip).astype(jnp.int32) != 1 - parity[0]
    slow = [jnp.where(odd, from_even[layer], from_odd[layer]) for layer in range(layers)]
    slow = [jnp.where(rows, value, 0.0) for value in slow]
    copies = []
    for block in range(columns // extent):
        at = slice(block * extent, (block + 1) * extent)
        far = covered(entry(slow_position, 1), block, (strip, extent))
        for layer in range(layers):
            value = staged[layer, :, at] + jnp.where(far, slow[layer], 0.0)
            final[layer, :, at] = value
        copy = pltpu.make_async_copy(final.at[:, :, at], out.at[:, :, at], sems.at[block])
        copy.start()
        copies.append(copy)
    for copy in copies:
        copy.wait()


def local(potential, probe, positions, intensity):
    layers, strip, columns = potential.shape
    extent = probe.shape[1]
    count = lax.axis_size("probe")
    depth_count = lax.axis_size("depth")
    assert positions.shape[0] == 1 and extent == 2 * strip and columns % extent == 0
    assert count % 2 == 0 and layers * (depth_count - 1) > 1
    slices = layers * depth_count
    half = (layers, strip, extent)
    field = (2, extent, extent)
    fast_pairs = [(i, i ^ 1) for i in range(count)]
    slow_pairs = [(i, (i + 1 if i % 2 else i - 1) % count) for i in range(count)]

    def step(x, by):
        return lax.ppermute(x, "probe", [(i, (i + by) % count) for i in range(count)])

    def to_depths(x):
        out = []
        for k in range(1, depth_count):
            pairs = [(i, (i + k) % depth_count) for i in range(depth_count)]
            out.append(lax.ppermute(x, "depth", pairs))
        return out

    def cut(shapes, position, *after):
        return call(cut_kernel, shapes, [], [position, tile, *after])

    place = lax.axis_index("depth").astype(jnp.int32).reshape(1)
    parity = (lax.axis_index("probe").astype(jnp.int32) & 1).reshape(1)
    prop, dft = [jnp.asarray(x) for x in tables(extent)]

    before = step(positions, 1)
    after = step(positions, -1)
    (tile,) = pl.pallas_call(
        tile_kernel,
        out_shape=[pltpu.VMEM(potential.shape, f32)],
        in_specs=[ANY],
        out_specs=[VMEM],
        scratch_shapes=[pltpu.SemaphoreType.DMA((layers,))],
        name="tile",
    )(potential)

    def by_layer(pieces, send):
        out = []
        for layer in range(layers):
            out.append(send(pieces[layer]))
        return out

    (for_before,) = cut([half], before)
    below = step(for_before, -1)
    (own,) = cut([half], positions, for_before)
    owns = to_depths(own)
    for_after = cut([half[1:]] * layers, after, own)
    above = by_layer(for_after, lambda x: step(x, 1))
    upper, wave = call(
        first_kernel,
        [(layers, 2, strip, extent), field],
        [positions],
        [probe, prop, own],
    )
    other = []
    for layer in range(layers):
        arrays = [positions, above[layer], below, wave]
        kernel = functools.partial(merge_kernel, layer)
        other += call(kernel, [half[1:]], [], arrays)
    others = by_layer(other, to_depths)
    wave, table, saved = call(
        functools.partial(enter_kernel, layers),
        [field, (slices, *field), (layers, *field)],
        [place],
        [wave, prop, upper, *other],
        aliases=[(0, 0)],
    )
    wave, table = call(
        functools.partial(middle_kernel, depth_count, layers),
        [field, table.shape],
        [place],
        [wave, prop, table, *owns, *others[0]],
        aliases=[(0, 0), (2, 1)],
    )
    rest = []
    for k in range(depth_count - 1):
        rest += [owns[k], *[others[layer][k] for layer in range(1, layers)]]

    def solve(turn, table, saved, *earlier):
        rest_refs = 6 + len(rest)
        return call(
            functools.partial(solve_kernel, depth_count, turn),
            [half, half, table.shape, saved.shape],
            [place, parity],
            [wave, saved, intensity, prop, dft, table, *rest, *earlier],
            aliases=[(5, 2), (1, 3)] + ([(rest_refs, 0)] if earlier else []),
            limit=4 * (depth_count - 1),
        )

    odd_groups = [(i, j) for i, j in slow_pairs if i % 2 == 1]
    even_groups = [fast_pairs[i] if i % 2 else slow_pairs[i] for i in range(count)]
    mine, outer, table, saved = solve(1, table, saved)
    from_odd = lax.ppermute(outer, "probe", odd_groups)
    mine, outer, _, _ = solve(0, table, saved, mine, outer)
    from_even = lax.ppermute(outer, "probe", even_groups)
    fast = lax.ppermute(outer, "probe", fast_pairs)
    odd = parity[0] == 1
    fast_position = jnp.where(odd, before, after)
    slow_position = jnp.where(odd, after, before)
    (staged,) = call(
        stage_kernel, [potential.shape], [parity], [positions, fast_position, mine, fast]
    )
    arrays = [slow_position, from_odd, from_even, staged]
    arrays = [pltpu.with_memory_space_constraint(x, pltpu.VMEM) for x in arrays]
    return pl.pallas_call(
        place_kernel,
        out_shape=jax.ShapeDtypeStruct(potential.shape, f32),
        in_specs=[SMEM] + [VMEM] * 4,
        out_specs=ANY,
        scratch_shapes=[
            pltpu.VMEM(potential.shape, f32),
            pltpu.SemaphoreType.DMA((columns // extent,)),
        ],
        name="place",
    )(parity, *arrays)


def solution(mesh):
    in_specs = (P("depth", "probe", None), P(), P("probe", None), P("probe", None, None))
    out_specs = P("depth", "probe", None)

    return jax.shard_map(
        local, mesh=mesh, in_specs=in_specs, out_specs=out_specs, check_vma=False
    )
```
